256 devices in a mesh: dp: 32 (over y, z_hi, core), ctx: 8 (over z_lo, x).
Axes of the slice: x: 4, y: 4, z: 8 (z_hi: 4, z_lo: 2; z = z_hi * 2 + z_lo), core: 2. Of those that a mesh axis runs over, the one named last changes fastest.
Arguments:
- q_feat: bfloat16 [16384, 4096], P('ctx', 'dp'), may hold values from -6 to 6
- k_feat: bfloat16 [16384, 4096], P('ctx', 'dp'), may hold values from -6 to 6
- v_feat: bfloat16 [16384, 4096], P('ctx', 'dp'), may hold values from -6 to 6
- short_taps: float32 [3, 4096], P(None, 'dp'), may hold values from -3 to 3
- skip_bias: float32 [4096], P('dp'), may hold values from -4 to 4
- freqs: float32 [32], replicated, may hold values from 1 to 8192
- phases: float32 [32], replicated, may hold values from -3.140625 to 3.140625
- w_first: float32 [32, 64], replicated, may hold values from -1 to 1
- b_first: float32 [64], replicated, may hold values from -4 to 4
- w_second: float32 [64, 64], replicated, may hold values from -0.75 to 0.75
- b_second: float32 [64], replicated, may hold values from -4 to 4
- w_out: float32 [64, 256], P(None, 'dp'), may hold values from -0.01171875 to 0.01171875
- rates: float32 [256], P('dp'), may hold values from 0.1 to 2
Outputs:
- gated_out: bfloat16 [16384, 4096], P('ctx', 'dp')
The draws below stay inside these ranges and needn't reach their ends.
All inputs are finite; a program needn't handle non-finite values.
Results may differ from the reference program's by a relative error of at most 0.0061.
Values may be sent and summed in bfloat16 or wider, within the bound.
A program may use at most 64 MiB of HBM per device.

```python
import math
import jax
import jax.numpy as jnp
from jax import lax

G = 256
GS = 16
D = 4096
EMB = 32
H = 64
BLK = 1024
SEQ = 16384


def level_of(rng, extent, split, smallest, largest):
    loudness = 1.0
    for dim, shards_of in split:
        heights = jax.random.uniform(jax.random.fold_in(jax.random.fold_in(rng, 6), dim), (shards_of,), jnp.float32, smallest / len(split), largest / len(split))
        loudness = loudness * jnp.repeat(jnp.exp(heights), extent[dim] // shards_of).reshape((-1,) + (1,) * (len(extent) - 1 - dim))
    return loudness


def bell_draw(key, shape, scale, most, cuts=(), kind=jnp.bfloat16):
    values = scale * jax.random.normal(key, shape, jnp.float32)
    if cuts:
        values = values * level_of(key, shape, cuts, -0.22, 0.18)
    return jnp.clip(values, -most, most).astype(kind)


def setup_inputs(seed: int = 0) -> dict:
    key_of = jax.random.split(jax.random.key(seed), 14)
    q_feat = bell_draw(key_of[0], (SEQ, D), 1.0, 6.0, ((0, 8), (1, 32)))
    k_feat = bell_draw(key_of[1], (SEQ, D), 1.0, 6.0, ((0, 8), (1, 32)))
    v_feat = bell_draw(key_of[2], (SEQ, D), 1.0, 6.0, ((0, 8), (1, 32)))
    short_taps = bell_draw(key_of[3], (3, D), 0.6, 3.0, ((1, 32),), jnp.float32)
    skip_bias = bell_draw(key_of[4], (D,), 1.0, 4.0, ((0, 32),), jnp.float32)
    freqs = jnp.clip(jnp.exp(jax.random.uniform(key_of[5], (EMB,), jnp.float32, math.log(1.0), math.log(8192.0))), 1.0, 8192.0)
    phases = jnp.clip(jax.random.uniform(key_of[6], (EMB,), jnp.float32, -3.140625, 3.140625), -3.140625, 3.140625)
    w_first = bell_draw(key_of[7], (EMB, H), EMB ** -0.5, 1.0, (), jnp.float32)
    b_first = bell_draw(key_of[8], (H,), 1.0, 4.0, (), jnp.float32)
    w_second = bell_draw(key_of[9], (H, H), H ** -0.5, 0.75, (), jnp.float32)
    b_second = bell_draw(key_of[10], (H,), 1.0, 4.0, (), jnp.float32)
    w_out = bell_draw(key_of[11], (H, G), (H * SEQ // 4) ** -0.5, 0.01171875, ((1, 32),), jnp.float32)
    rates = jnp.clip(jnp.exp(math.log(2.0) - 2.9957323 * jax.random.uniform(key_of[12], (G,), jnp.float32) ** level_of(key_of[12], (G,), ((0, 32),), -0.2, 0.2)), 0.1, 2.0)
    return {"q_feat": q_feat, "k_feat": k_feat, "v_feat": v_feat, "short_taps": short_taps, "skip_bias": skip_bias, "freqs": freqs, "phases": phases, "w_first": w_first, "b_first": b_first, "w_second": w_second, "b_second": b_second, "w_out": w_out, "rates": rates}


MAXIMUM_ACCURACY = lax.Precision.HIGHEST


def angle_table(row_count, col_count, offset, block_len):
    row_ids = jnp.arange(row_count, dtype=jnp.int32)[:, None] + offset
    col_ids = jnp.arange(col_count, dtype=jnp.int32)[None, :]
    return (math.pi / block_len) * ((row_ids * col_ids) % (2 * block_len)).astype(jnp.float32)


def forward_tables(block_len, col_count):
    angles = angle_table(block_len, col_count, 0, block_len)
    first_row = jnp.arange(block_len, dtype=jnp.int32)[:, None] == 0
    alternate = (1 - 2 * (jnp.arange(col_count, dtype=jnp.int32) % 2)).astype(jnp.float32)[None, :]
    return jnp.cos(angles), jnp.where(first_row, alternate, -jnp.sin(angles))


def inverse_tables(block_len):
    angles = angle_table(block_len, block_len, block_len, block_len)
    first_col = jnp.arange(block_len, dtype=jnp.int32)[None, :] == 0
    alternate = (1 - 2 * ((block_len + jnp.arange(block_len, dtype=jnp.int32)) % 2)).astype(jnp.float32)[:, None]
    real_part = jnp.where(first_col, 0.5 / block_len, jnp.cos(angles) / block_len)
    imag_part = jnp.where(first_col, alternate * (0.5 / block_len), -jnp.sin(angles) / block_len)
    return real_part, imag_part


def hidden_layers(positions, seq_len, freqs, phases, w_first, b_first, w_second, b_second):
    scaled = positions[:, None] / seq_len
    feature = jnp.sin(2.0 * math.pi * freqs[None, :] * scaled + phases[None, :])
    first_layer = jnp.sin(jnp.dot(feature, w_first, precision=MAXIMUM_ACCURACY) + b_first)
    return jnp.sin(jnp.dot(first_layer, w_second, precision=MAXIMUM_ACCURACY) + b_second)


def filter_rows(second, seq_len, w_cols, rate_cols):
    positions = jnp.arange(seq_len, dtype=jnp.int32).astype(jnp.float32)
    values = jnp.einsum("ph,hg->gp", second, w_cols, precision=MAXIMUM_ACCURACY)
    return values * jnp.exp(-rate_cols[:, None] * (positions[None, :] / seq_len))


def lag_spectra(filter_table, block_len, block_count):
    wide_re, wide_im = forward_tables(block_len, 2 * block_len)
    wide_re = wide_re.astype(jnp.bfloat16).astype(jnp.float32)
    wide_im = wide_im.astype(jnp.bfloat16).astype(jnp.float32)
    col_count = filter_table.shape[0]
    rounded = filter_table.astype(jnp.bfloat16).astype(jnp.float32)
    padded = jnp.concatenate([jnp.zeros((col_count, block_len), jnp.float32), rounded], 1)
    padded = padded.reshape(col_count, block_count + 1, block_len)
    spec_real = jnp.einsum("km,gjm->jgk", wide_re[:, :block_len], padded[:, :-1], precision=MAXIMUM_ACCURACY)
    spec_real = spec_real + jnp.einsum("km,gjm->jgk", wide_re[:, block_len:], padded[:, 1:], precision=MAXIMUM_ACCURACY)
    spec_imag = jnp.einsum("km,gjm->jgk", wide_im[:, :block_len], padded[:, :-1], precision=MAXIMUM_ACCURACY)
    spec_imag = spec_imag + jnp.einsum("km,gjm->jgk", wide_im[:, block_len:], padded[:, 1:], precision=MAXIMUM_ACCURACY)
    return spec_real, spec_imag


def expand(blocks, group_size):
    return jnp.repeat(jnp.swapaxes(blocks, -1, -2), group_size, axis=-1)


def accumulate(totals, pieces, filters, live_rows):
    total_re, total_im = totals
    part_re = pieces[0].astype(jnp.float32)
    part_im = pieces[1].astype(jnp.float32)
    filter_re, filter_im = filters
    total_re = total_re + (part_re * filter_re - live_rows * (part_im * filter_im))
    total_im = total_im + (live_rows * (part_re * filter_im + part_im * filter_re) + (1.0 - live_rows) * (part_im * filter_im))
    return total_re, total_im


def reference(q_feat, k_feat, v_feat, short_taps, skip_bias, freqs, phases, w_first, b_first, w_second, b_second, w_out, rates):
    block_len = BLK
    block_count = SEQ // BLK
    channels = D
    positions = jnp.arange(SEQ, dtype=jnp.int32).astype(jnp.float32)
    second = hidden_layers(positions, SEQ, freqs, phases, w_first, b_first, w_second, b_second)
    filter_table = filter_rows(second, SEQ, w_out, rates)
    spec_re, spec_im = lag_spectra(filter_table, block_len, block_count)
    narrow = forward_tables(block_len, block_len)
    twiddle_real = narrow[0].astype(jnp.bfloat16)
    twiddle_imaginary = narrow[1].astype(jnp.bfloat16)
    back = inverse_tables(block_len)
    inverse_real = back[0].astype(jnp.bfloat16)
    inverse_imaginary = back[1].astype(jnp.bfloat16)
    live_rows = (jnp.arange(block_len, dtype=jnp.int32) >= 1).astype(jnp.float32)[:, None]

    extended = jnp.concatenate([jnp.zeros((2, channels), jnp.float32), v_feat.astype(jnp.float32)], 0)
    smoothed = short_taps[0] * extended[2:] + short_taps[1] * extended[1:-1] + short_taps[2] * extended[:-2]
    signal = (k_feat.astype(jnp.float32) * smoothed).astype(jnp.bfloat16)
    block_pieces = signal.reshape(block_count, block_len, channels).astype(jnp.float32)
    input_real = jnp.einsum("rl,jlq->jrq", twiddle_real.astype(jnp.float32), block_pieces, precision=MAXIMUM_ACCURACY).astype(jnp.bfloat16)
    input_imaginary = jnp.einsum("rl,jlq->jrq", twiddle_imaginary.astype(jnp.float32), block_pieces, precision=MAXIMUM_ACCURACY).astype(jnp.bfloat16)
    pieces = []
    for target in range(block_count):
        totals = (jnp.zeros((block_len, channels), jnp.float32), jnp.zeros((block_len, channels), jnp.float32))
        for lag_index in range(target + 1):
            filters = (expand(spec_re[lag_index], GS), expand(spec_im[lag_index], GS))
            totals = accumulate(totals, (input_real[target - lag_index], input_imaginary[target - lag_index]), filters, live_rows)
        conv_block = jnp.dot(inverse_real, totals[0].astype(jnp.bfloat16), preferred_element_type=jnp.float32)
        conv_block = conv_block + jnp.dot(inverse_imaginary, totals[1].astype(jnp.bfloat16), preferred_element_type=jnp.float32)
        pieces.append(conv_block)
    conv = jnp.concatenate(pieces, 0)
    return (q_feat.astype(jnp.float32) * (conv + skip_bias * signal.astype(jnp.float32))).astype(jnp.bfloat16)
```

```python
import functools
import math

import jax
import jax.numpy as jnp
from jax import lax
from jax.experimental import pallas as pl
from jax.experimental.pallas import tpu as pltpu
from jax.sharding import PartitionSpec as P

MESH = pl.DeviceIdType.MESH
F32 = jnp.float32
BF16 = jnp.bfloat16
HIGHEST = lax.Precision.HIGHEST

TB = 256
CHAIN = 16

PI_A = 3.140625
PI_B = 9.67025756835938e-04
PI_C = 6.277114152908325e-07


def sine(x):
    turns = jnp.floor(x * (1.0 / math.pi) + 0.5)
    r = ((x - turns * PI_A) - turns * PI_B) - turns * PI_C
    odd = turns - 2.0 * jnp.floor(turns * 0.5)
    r = r * (1.0 - 2.0 * odd)
    r2 = r * r
    tail = -2.5052108e-8 + r2 * 1.6059044e-10
    tail = 2.7557319e-6 + r2 * tail
    tail = -1.9841270e-4 + r2 * tail
    tail = 8.3333333e-3 + r2 * tail
    tail = -1.6666667e-1 + r2 * tail
    return r + r * r2 * tail


def column(row):
    n = row.shape[1]
    square = jnp.broadcast_to(row, (n, n))
    at_row = lax.broadcasted_iota(jnp.int32, (n, n), 0)
    at_col = lax.broadcasted_iota(jnp.int32, (n, n), 1)
    return jnp.sum(jnp.where(at_row == at_col, square, 0.0), axis=1, keepdims=True)


def rows_to_rows(a, b):
    return lax.dot_general(
        a, b, (((0,), (0,)), ((), ())), precision=HIGHEST, preferred_element_type=F32
    )


def kernel(
    n,
    span,
    groups,
    size,
    q_hbm,
    k_hbm,
    v_hbm,
    taps_ref,
    skip_ref,
    freqs_ref,
    phases_ref,
    w1_ref,
    b1_ref,
    w2_ref,
    b2_ref,
    wo_ref,
    rates_ref,
    o_hbm,
    q_ref,
    k_ref,
    v_ref,
    o_ref,
    halo_ref,
    ext_ref,
    sig_ref,
    xs_ref,
    xa_ref,
    hs_ref,
    ha_ref,
    f_ref,
    acc_ref,
    ys_ref,
    yr_ref,
    in_sem,
    out_sem,
    halo_send,
    halo_recv,
    x_send,
    x_recv,
    h_send,
    h_recv,
    y_send,
    y_recv,
):
    me = lax.axis_index("ctx")
    seq = span * n
    blocks = span // TB
    piece = blocks * size
    pad = CHAIN * size

    def peer(j):
        return lax.rem(me + j, n)

    def source(j):
        return lax.rem(me + (n - j), n)

    load_v = pltpu.make_async_copy(v_hbm, v_ref, in_sem.at[0])
    load_k = pltpu.make_async_copy(k_hbm, k_ref, in_sem.at[1])
    load_q = pltpu.make_async_copy(q_hbm, q_ref, in_sem.at[2])
    load_v.start()
    load_k.start()
    load_q.start()

    barrier = pltpu.get_barrier_semaphore()
    for j in range(1, n):
        pl.semaphore_signal(
            barrier, inc=1, device_id={"ctx": peer(j)}, device_id_type=MESH
        )
    pl.semaphore_wait(barrier, n - 1)

    load_v.wait()
    halo = pltpu.make_async_remote_copy(
        src_ref=v_ref.at[pl.ds(span - 16, 16), :],
        dst_ref=halo_ref,
        send_sem=halo_send,
        recv_sem=halo_recv,
        device_id={"ctx": peer(1)},
        device_id_type=MESH,
    )
    halo.start()
    ext_ref[8:, :] = v_ref[...].astype(F32)
    load_k.wait()
    halo.wait()
    ext_ref[0:8, :] = jnp.where(me > 0, halo_ref[8:16, :].astype(F32), 0.0)

    taps = taps_ref[...]

    def one_block(a, _):
        at = pl.multiple_of(a * TB, TB)
        mixed = taps[0:1] * ext_ref[pl.ds(at + 8, TB), :]
        mixed = mixed + taps[1:2] * ext_ref[pl.ds(at + 7, TB), :]
        mixed = mixed + taps[2:3] * ext_ref[pl.ds(at + 6, TB), :]
        signal = (k_ref[pl.ds(at, TB), :].astype(F32) * mixed).astype(BF16)
        sig_ref[pl.ds(at, TB), :] = signal
        turned = signal.astype(F32).T.astype(BF16)
        row = pl.multiple_of(a * size, size)
        for g in range(groups):
            xs_ref[g, pl.ds(row, size), :] = turned[g * size : (g + 1) * size]
        return 0

    lax.fori_loop(0, blocks, one_block, 0)

    def x_copy(j):
        return pltpu.make_async_remote_copy(
            src_ref=xs_ref.at[peer(j)],
            dst_ref=xa_ref.at[pl.ds(pl.multiple_of(pad + me * piece, 16), piece), :],
            send_sem=x_send.at[j],
            recv_sem=x_recv.at[j],
            device_id={"ctx": peer(j)},
            device_id_type=MESH,
        )

    for j in range(1, n):
        x_copy(j).start()
    xa_ref[0:pad, :] = jnp.zeros((pad, TB), BF16)
    xa_ref[pl.ds(pl.multiple_of(pad + me * piece, 16), piece), :] = xs_ref[me]

    freq = column(freqs_ref[...]) * (2.0 * math.pi)
    phase = column(phases_ref[...])
    bias1 = column(b1_ref[...])
    bias2 = column(b2_ref[...])
    rate = column(rates_ref[...])
    wide = 512

    def some_positions(i, _):
        start = me * span + i * wide
        lanes = lax.broadcasted_iota(jnp.int32, (1, wide), 1) + start
        scaled = lanes.astype(F32) / seq
        feature = sine(freq * scaled + phase)
        first = sine(rows_to_rows(w1_ref[...], feature) + bias1)
        second = sine(rows_to_rows(w2_ref[...], first) + bias2)
        values = rows_to_rows(wo_ref[...], second) * jnp.exp(-rate * scaled)
        for t in range(wide // 128):
            for g in range(groups):
                hs_ref[g, pl.ds(i * (wide // 128) + t, 1), :] = values[
                    g : g + 1, t * 128 : (t + 1) * 128
                ]
        return 0

    lax.fori_loop(0, span // wide, some_positions, 0)

    tiles = span // 128

    def h_copy(j):
        return pltpu.make_async_remote_copy(
            src_ref=hs_ref.at[peer(j)],
            dst_ref=ha_ref.at[pl.ds(pl.multiple_of(me * tiles, 8), tiles), :],
            send_sem=h_send.at[j],
            recv_sem=h_recv.at[j],
            device_id={"ctx": peer(j)},
            device_id_type=MESH,
        )

    for j in range(1, n):
        h_copy(j).start()
    ha_ref[pl.ds(pl.multiple_of(me * tiles, 8), tiles), :] = hs_ref[me]
    for j in range(1, n):
        h_copy(j).wait()

    at_row = lax.broadcasted_iota(jnp.int32, (128, 128), 0)
    at_col = lax.broadcasted_iota(jnp.int32, (128, 128), 1)
    keep = at_col >= at_row
    f_ref[0] = jnp.zeros((128, 128), BF16)

    def one_tile(t, before):
        row = jnp.broadcast_to(ha_ref[pl.ds(t, 1), :], (128, 128))
        turned = pltpu.roll(row, 0, 1, stride=1, stride_axis=0)
        f_ref[t + 1] = jnp.where(keep, turned, before).astype(BF16)
        return turned

    lax.fori_loop(0, seq // 128, one_tile, jnp.zeros((128, 128), F32), unroll=2)

    for j in range(1, n):
        x_copy(j).wait()

    def lag_block(lag):
        low, mid, high = f_ref[2 * lag], f_ref[2 * lag + 1], f_ref[2 * lag + 2]
        return jnp.concatenate(
            [jnp.concatenate([mid, high], 1), jnp.concatenate([low, mid], 1)], 0
        )

    def y_copy(k, to, half, tile):
        j = lax.rem(to - me + n, n)
        return pltpu.make_async_remote_copy(
            src_ref=ys_ref.at[tile, pl.ds(half * piece, piece), :],
            dst_ref=yr_ref.at[me],
            send_sem=y_send.at[j],
            recv_sem=y_recv.at[j],
            device_id={"ctx": to},
            device_id_type=MESH,
        )

    tile_count = n // 2
    mine = me // 2
    half_me = lax.rem(me, 2)
    for k in range(tile_count):
        tile = lax.rem(mine + 1 + k, tile_count)
        acc_ref[...] = jnp.zeros_like(acc_ref)

        def lag_group(i, _, tile=tile):
            left, right = [], []
            for c in range(CHAIN):
                start = pad + (tile - i) * (2 * piece) - c * size
                left.append(xa_ref[pl.ds(pl.multiple_of(start, 16), 2 * piece), :])
                right.append(lag_block(i * CHAIN + c))
            acc_ref[...] += jnp.dot(
                jnp.concatenate(left, 1),
                jnp.concatenate(right, 0),
                preferred_element_type=F32,
            )
            return 0

        lax.fori_loop(0, tile + 1, lag_group, 0)
        ys_ref[tile] = acc_ref[...].astype(BF16)
        if k < tile_count - 1:
            y_copy(k, 2 * tile, 0, tile).start()
            y_copy(k, 2 * tile + 1, 1, tile).start()
        else:
            y_copy(k, 2 * tile + 1 - half_me, 1 - half_me, tile).start()
            yr_ref[me] = ys_ref[
                tile, pl.ds(pl.multiple_of(half_me * piece, 16), piece), :
            ]

    load_q.wait()
    for j in range(1, n):
        pltpu.make_async_remote_copy(
            src_ref=ys_ref.at[0, pl.ds(0, piece), :],
            dst_ref=yr_ref.at[source(j)],
            send_sem=y_send.at[j],
            recv_sem=y_recv.at[j],
            device_id={"ctx": peer(j)},
            device_id_type=MESH,
        ).wait()

    skip = skip_ref[...]

    def last_block(a, _):
        at = pl.multiple_of(a * TB, TB)
        row = pl.multiple_of(a * size, size)
        turned = jnp.concatenate(
            [yr_ref[g, pl.ds(row, size), :] for g in range(groups)], 0
        )
        conv = turned.astype(F32).T
        total = conv + skip * sig_ref[pl.ds(at, TB), :].astype(F32)
        o_ref[pl.ds(at, TB), :] = (
            q_ref[pl.ds(at, TB), :].astype(F32) * total
        ).astype(BF16)
        return 0

    lax.fori_loop(0, blocks, last_block, 0)
    store = pltpu.make_async_copy(o_ref, o_hbm, out_sem)
    store.start()
    store.wait()


def on_device(
    q_feat,
    k_feat,
    v_feat,
    short_taps,
    skip_bias,
    freqs,
    phases,
    w_first,
    b_first,
    w_second,
    b_second,
    w_out,
    rates,
):
    n = lax.axis_size("ctx")
    span, channels = q_feat.shape
    groups = rates.shape[0]
    size = channels // groups
    seq = span * n
    blocks = span // TB
    piece = blocks * size
    pad = CHAIN * size
    hbm = pl.BlockSpec(memory_space=pl.ANY)
    vmem = pl.BlockSpec(memory_space=pltpu.VMEM)
    dma = pltpu.SemaphoreType.DMA
    return pl.pallas_call(
        functools.partial(kernel, n, span, groups, size),
        name="toeplitz_conv",
        out_shape=jax.ShapeDtypeStruct((span, channels), BF16),
        in_specs=[hbm] * 3 + [vmem] * 10,
        out_specs=hbm,
        scratch_shapes=[
            pltpu.VMEM((span, channels), BF16),
            pltpu.VMEM((span, channels), BF16),
            pltpu.VMEM((span, channels), BF16),
            pltpu.VMEM((span, channels), BF16),
            pltpu.VMEM((16, channels), BF16),
            pltpu.VMEM((span + 8, channels), F32),
            pltpu.VMEM((span, channels), BF16),
            pltpu.VMEM((groups, piece, TB), BF16),
            pltpu.VMEM((pad + n * piece, TB), BF16),
            pltpu.VMEM((groups, span // 128, 128), F32),
            pltpu.VMEM((seq // 128, 128), F32),
            pltpu.VMEM((seq // 128 + 1, 128, 128), BF16),
            pltpu.VMEM((2 * piece, TB), F32),
            pltpu.VMEM((n // 2, 2 * piece, TB), BF16),
            pltpu.VMEM((groups, piece, TB), BF16),
            dma((3,)),
            dma,
            dma,
            dma,
            dma((n,)),
            dma((n,)),
            dma((n,)),
            dma((n,)),
            dma((n,)),
            dma((n,)),
        ],
        compiler_params=pltpu.CompilerParams(
            collective_id=0, has_side_effects=True, vmem_limit_bytes=40 << 20
        ),
    )(
        q_feat,
        k_feat,
        v_feat,
        short_taps,
        skip_bias.reshape(1, -1),
        freqs.reshape(1, -1),
        phases.reshape(1, -1),
        w_first,
        b_first.reshape(1, -1),
        w_second,
        b_second.reshape(1, -1),
        w_out,
        rates.reshape(1, -1),
    )


def solution(mesh):
    return jax.shard_map(
        on_device,
        mesh=mesh,
        in_specs=(
            P("ctx", "dp"),
            P("ctx", "dp"),
            P("ctx", "dp"),
            P(None, "dp"),
            P("dp"),
            P(),
            P(),
            P(),
            P(),
            P(),
            P(),
            P(None, "dp"),
            P("dp"),
        ),
        out_specs=P("ctx", "dp"),
        check_vma=False,
    )
```

```python
import functools
import math

import jax
import jax.numpy as jnp
from jax import lax
from jax.experimental import pallas as pl
from jax.experimental.pallas import tpu as pltpu
from jax.sharding import PartitionSpec as P

MESH = pl.DeviceIdType.MESH
F32 = jnp.float32
BF16 = jnp.bfloat16
HIGHEST = lax.Precision.HIGHEST

TB = 256
CHAIN = 16

PI_A = 3.140625
PI_B = 9.67025756835938e-04
PI_C = 6.277114152908325e-07


def sine(x):
    turns = jnp.floor(x * (1.0 / math.pi) + 0.5)
    r = ((x - turns * PI_A) - turns * PI_B) - turns * PI_C
    odd = turns - 2.0 * jnp.floor(turns * 0.5)
    r = r * (1.0 - 2.0 * odd)
    r2 = r * r
    tail = -2.5052108e-8 + r2 * 1.6059044e-10
    tail = 2.7557319e-6 + r2 * tail
    tail = -1.9841270e-4 + r2 * tail
    tail = 8.3333333e-3 + r2 * tail
    tail = -1.6666667e-1 + r2 * tail
    return r + r * r2 * tail


def column(row):
    n = row.shape[1]
    square = jnp.broadcast_to(row, (n, n))
    at_row = lax.broadcasted_iota(jnp.int32, (n, n), 0)
    at_col = lax.broadcasted_iota(jnp.int32, (n, n), 1)
    return jnp.sum(jnp.where(at_row == at_col, square, 0.0), axis=1, keepdims=True)


def rows_to_rows(a, b):
    return lax.dot_general(
        a, b, (((0,), (0,)), ((), ())), precision=HIGHEST, preferred_element_type=F32
    )


def kernel(
    n,
    span,
    groups,
    size,
    q_hbm,
    k_hbm,
    v_hbm,
    taps_hbm,
    skip_hbm,
    freqs_hbm,
    phases_hbm,
    w1_hbm,
    b1_hbm,
    w2_hbm,
    b2_hbm,
    wo_hbm,
    rates_hbm,
    o_ref,
    taps_ref,
    skip_ref,
    freqs_ref,
    phases_ref,
    w1_ref,
    b1_ref,
    w2_ref,
    b2_ref,
    wo_ref,
    rates_ref,
    q_ref,
    k_ref,
    v_ref,
    halo_ref,
    ext_ref,
    sig_ref,
    xs_ref,
    xa_ref,
    hs_ref,
    ha_ref,
    f_ref,
    ys_ref,
    yr_ref,
    in_sem,
    small_sem,
    halo_send,
    halo_recv,
    x_send,
    x_recv,
    h_send,
    h_recv,
    y_send,
    y_recv,
):
    me = lax.axis_index("ctx")
    seq = span * n
    blocks = span // TB
    piece = blocks * size
    pad = CHAIN * size

    def peer(j):
        return lax.rem(me + j, n)

    def source(j):
        return lax.rem(me + (n - j), n)

    load_v = pltpu.make_async_copy(v_hbm, v_ref, in_sem.at[0])
    load_k = pltpu.make_async_copy(k_hbm, k_ref, in_sem.at[1])
    load_q = pltpu.make_async_copy(q_hbm, q_ref, in_sem.at[2])
    load_v.start()
    load_k.start()
    loads = [
        pltpu.make_async_copy(src, dst, small_sem.at[i])
        for i, (src, dst) in enumerate(
            [
                (taps_hbm, taps_ref),
                (skip_hbm, skip_ref),
                (freqs_hbm, freqs_ref),
                (phases_hbm, phases_ref),
                (w1_hbm, w1_ref),
                (b1_hbm, b1_ref),
                (w2_hbm, w2_ref),
                (b2_hbm, b2_ref),
                (wo_hbm, wo_ref),
                (rates_hbm, rates_ref),
            ]
        )
    ]
    barrier = pltpu.get_barrier_semaphore()
    for j in range(1, n):
        pl.semaphore_signal(
            barrier, inc=1, device_id={"ctx": peer(j)}, device_id_type=MESH
        )
    for load in loads:
        load.start()
    load_q.start()

    load_v.wait()
    ext_ref[8:, :] = v_ref[...].astype(F32)
    ext_ref[0:8, :] = jnp.zeros((8, groups * size), F32)
    loads[0].wait()
    load_k.wait()
    taps = taps_ref[...]

    def one_block(a, _):
        at = pl.multiple_of(a * TB, TB)
        mixed = taps[0:1] * ext_ref[pl.ds(at + 8, TB), :]
        mixed = mixed + taps[1:2] * ext_ref[pl.ds(at + 7, TB), :]
        mixed = mixed + taps[2:3] * ext_ref[pl.ds(at + 6, TB), :]
        signal = (k_ref[pl.ds(at, TB), :].astype(F32) * mixed).astype(BF16)
        sig_ref[pl.ds(at, TB), :] = signal
        turned = signal.astype(F32).T.astype(BF16)
        row = pl.multiple_of(a * size, size)
        for g in range(groups):
            xs_ref[g, pl.ds(row, size), :] = turned[g * size : (g + 1) * size]
        return 0

    lax.fori_loop(1, blocks, one_block, 0)
    pl.semaphore_wait(barrier, n - 1)

    halo = pltpu.make_async_remote_copy(
        src_ref=v_ref.at[pl.ds(span - 16, 16), :],
        dst_ref=halo_ref,
        send_sem=halo_send,
        recv_sem=halo_recv,
        device_id={"ctx": peer(1)},
        device_id_type=MESH,
    )
    halo.start()

    half = piece // 2

    def x_copy(j, part):
        at = pad + me * piece + part * half
        return pltpu.make_async_remote_copy(
            src_ref=xs_ref.at[peer(j), pl.ds(part * half, half), :],
            dst_ref=xa_ref.at[pl.ds(pl.multiple_of(at, 16), half), :],
            send_sem=x_send.at[part, j],
            recv_sem=x_recv.at[part, j],
            device_id={"ctx": peer(j)},
            device_id_type=MESH,
        )

    for j in range(1, n):
        x_copy(j, 1).start()
    xa_ref[0:pad, :] = jnp.zeros((pad, TB), BF16)
    halo.wait()
    ext_ref[0:8, :] = jnp.where(me > 0, halo_ref[8:16, :].astype(F32), 0.0)
    one_block(0, 0)
    for j in range(1, n):
        x_copy(j, 0).start()
    xa_ref[pl.ds(pl.multiple_of(pad + me * piece, 16), piece), :] = xs_ref[me]

    for load in loads[1:]:
        load.wait()
    freq = column(freqs_ref[...]) * (2.0 * math.pi)
    phase = column(phases_ref[...])
    bias1 = column(b1_ref[...])
    bias2 = column(b2_ref[...])
    rate = column(rates_ref[...])
    wide = 512

    def some_positions(i, _):
        start = me * span + i * wide
        lanes = lax.broadcasted_iota(jnp.int32, (1, wide), 1) + start
        scaled = lanes.astype(F32) / seq
        feature = sine(freq * scaled + phase)
        first = sine(rows_to_rows(w1_ref[...], feature) + bias1)
        second = sine(rows_to_rows(w2_ref[...], first) + bias2)
        values = lax.dot(
            wo_ref[...], second, precision=HIGHEST, preferred_element_type=F32
        ) * jnp.exp(-rate * scaled)
        for t in range(wide // 128):
            for g in range(groups):
                hs_ref[g, pl.ds(i * (wide // 128) + t, 1), :] = values[
                    g : g + 1, t * 128 : (t + 1) * 128
                ]
        return 0

    lax.fori_loop(0, span // wide, some_positions, 0)

    tiles = span // 128

    def h_copy(j):
        return pltpu.make_async_remote_copy(
            src_ref=hs_ref.at[peer(j)],
            dst_ref=ha_ref.at[pl.ds(pl.multiple_of(me * tiles, 8), tiles), :],
            send_sem=h_send.at[j],
            recv_sem=h_recv.at[j],
            device_id={"ctx": peer(j)},
            device_id_type=MESH,
        )

    for j in range(1, n):
        h_copy(j).start()
    ha_ref[pl.ds(pl.multiple_of(me * tiles, 8), tiles), :] = hs_ref[me]
    for j in range(1, n):
        h_copy(j).wait()

    at_row = lax.broadcasted_iota(jnp.int32, (128, 128), 0)
    at_col = lax.broadcasted_iota(jnp.int32, (128, 128), 1)
    keep = at_col >= at_row
    f_ref[0] = jnp.zeros((128, 128), BF16)

    def one_tile(t, before):
        row = jnp.broadcast_to(ha_ref[pl.ds(t, 1), :], (128, 128))
        turned = pltpu.roll(row, 0, 1, stride=1, stride_axis=0)
        f_ref[t + 1] = jnp.where(keep, turned, before).astype(BF16)
        return turned

    lax.fori_loop(0, seq // 128, one_tile, jnp.zeros((128, 128), F32), unroll=32)

    def x_wait(s):
        j = lax.rem(me - s + n, n)
        for part in (1, 0):
            at = pad + s * piece + part * half
            pltpu.make_async_remote_copy(
                src_ref=xs_ref.at[s, pl.ds(part * half, half), :],
                dst_ref=xa_ref.at[pl.ds(pl.multiple_of(at, 16), half), :],
                send_sem=x_send.at[part, j],
                recv_sem=x_recv.at[part, j],
                device_id={"ctx": s},
                device_id_type=MESH,
            ).wait_recv()

    def lag_block(lag):
        low, mid, high = f_ref[2 * lag], f_ref[2 * lag + 1], f_ref[2 * lag + 2]
        return jnp.concatenate(
            [jnp.concatenate([mid, high], 1), jnp.concatenate([low, mid], 1)], 0
        )

    def y_copy(to):
        j = lax.rem(to - me + n, n)
        return pltpu.make_async_remote_copy(
            src_ref=ys_ref.at[to],
            dst_ref=yr_ref.at[me],
            send_sem=y_send.at[j],
            recv_sem=y_recv.at[j],
            device_id={"ctx": to},
            device_id_type=MESH,
        )

    def one_source(s, _):
        x_wait(s)
        return 0

    lax.fori_loop(0, me, one_source, 0)

    def one_span(k, _):
        to = lax.rem(me + 1 + k, n)

        @pl.when(to > me)
        def _():
            x_wait(to)

        for c in range(n):

            @pl.when(to == c)
            def _(c=c):
                left, right = [], []
                for lag in range((c + 1) * blocks):
                    start = pad + c * piece - lag * size
                    if start + piece <= pad:
                        break
                    left.append(xa_ref[start : start + piece, :])
                    right.append(lag_block(lag))
                ys_ref[c] = jnp.dot(
                    jnp.concatenate(left, 1),
                    jnp.concatenate(right, 0),
                    preferred_element_type=F32,
                ).astype(BF16)

        @pl.when(to != me)
        def _():
            y_copy(to).start()

        return 0

    lax.fori_loop(0, n, one_span, 0)
    yr_ref[me] = ys_ref[me]
    for j in range(1, n):
        for part in (1, 0):
            x_copy(j, part).wait_send()

    load_q.wait()
    for j in range(1, n):
        pltpu.make_async_remote_copy(
            src_ref=ys_ref.at[peer(j)],
            dst_ref=yr_ref.at[source(j)],
            send_sem=y_send.at[j],
            recv_sem=y_recv.at[j],
            device_id={"ctx": peer(j)},
            device_id_type=MESH,
        ).wait()

    skip = skip_ref[...]

    def last_block(a, _):
        at = pl.multiple_of(a * TB, TB)
        row = pl.multiple_of(a * size, size)
        turned = jnp.concatenate(
            [yr_ref[g, pl.ds(row, size), :] for g in range(groups)], 0
        )
        conv = turned.astype(F32).T
        total = conv + skip * sig_ref[pl.ds(at, TB), :].astype(F32)
        o_ref[pl.ds(at, TB), :] = (
            q_ref[pl.ds(at, TB), :].astype(F32) * total
        ).astype(BF16)
        return 0

    lax.fori_loop(0, blocks, last_block, 0)


def on_device(
    q_feat,
    k_feat,
    v_feat,
    short_taps,
    skip_bias,
    freqs,
    phases,
    w_first,
    b_first,
    w_second,
    b_second,
    w_out,
    rates,
):
    n = lax.axis_size("ctx")
    span, channels = q_feat.shape
    groups = rates.shape[0]
    size = channels // groups
    seq = span * n
    blocks = span // TB
    piece = blocks * size
    pad = CHAIN * size
    hbm = pl.BlockSpec(memory_space=pl.ANY)
    vmem = pl.BlockSpec(memory_space=pltpu.VMEM)
    dma = pltpu.SemaphoreType.DMA
    return pl.pallas_call(
        functools.partial(kernel, n, span, groups, size),
        name="toeplitz_conv",
        out_shape=jax.ShapeDtypeStruct((span, channels), BF16),
        in_specs=[hbm] * 13,
        out_specs=vmem,
        scratch_shapes=[
            pltpu.VMEM(short_taps.shape, F32),
            pltpu.VMEM((1, channels), F32),
            pltpu.VMEM((1, freqs.shape[0]), F32),
            pltpu.VMEM((1, phases.shape[0]), F32),
            pltpu.VMEM(w_first.shape, F32),
            pltpu.VMEM((1, b_first.shape[0]), F32),
            pltpu.VMEM(w_second.shape, F32),
            pltpu.VMEM((1, b_second.shape[0]), F32),
            pltpu.VMEM((groups, w_out.shape[0]), F32),
            pltpu.VMEM((1, groups), F32),
            pltpu.VMEM((span, channels), BF16),
            pltpu.VMEM((span, channels), BF16),
            pltpu.VMEM((span, channels), BF16),
            pltpu.VMEM((16, channels), BF16),
            pltpu.VMEM((span + 8, channels), F32),
            pltpu.VMEM((span, channels), BF16),
            pltpu.VMEM((groups, piece, TB), BF16),
            pltpu.VMEM((pad + n * piece, TB), BF16),
            pltpu.VMEM((groups, span // 128, 128), F32),
            pltpu.VMEM((seq // 128, 128), F32),
            pltpu.VMEM((seq // 128 + 1, 128, 128), BF16),
            pltpu.VMEM((n, piece, TB), BF16),
            pltpu.VMEM((groups, piece, TB), BF16),
            dma((3,)),
            dma((10,)),
            dma,
            dma,
            dma((2, n)),
            dma((2, n)),
            dma((n,)),
            dma((n,)),
            dma((n,)),
            dma((n,)),
        ],
        compiler_params=pltpu.CompilerParams(
            collective_id=0, has_side_effects=True, vmem_limit_bytes=62 << 20
        ),
    )(
        q_feat,
        k_feat,
        v_feat,
        short_taps,
        skip_bias.reshape(1, -1),
        freqs.reshape(1, -1),
        phases.reshape(1, -1),
        w_first,
        b_first.reshape(1, -1),
        w_second,
        b_second.reshape(1, -1),
        w_out.T,
        rates.reshape(1, -1),
    )


def solution(mesh):
    return jax.shard_map(
        on_device,
        mesh=mesh,
        in_specs=(
            P("ctx", "dp"),
            P("ctx", "dp"),
            P("ctx", "dp"),
            P(None, "dp"),
            P("dp"),
            P(),
            P(),
            P(),
            P(),
            P(),
            P(),
            P(None, "dp"),
            P("dp"),
        ),
        out_specs=P("ctx", "dp"),
        check_vma=False,
    )
```

```python
import functools
import math

import jax
import jax.numpy as jnp
from jax import lax
from jax.experimental import pallas as pl
from jax.experimental.pallas import tpu as pltpu
from jax.sharding import PartitionSpec as P

MESH = pl.DeviceIdType.MESH
F32 = jnp.float32
BF16 = jnp.bfloat16
HIGHEST = lax.Precision.HIGHEST

TB = 256
CHAIN = 16

PI_A = 3.140625
PI_B = 9.67025756835938e-04
PI_C = 6.277114152908325e-07


def sine(x):
    turns = jnp.floor(x * (1.0 / math.pi) + 0.5)
    r = ((x - turns * PI_A) - turns * PI_B) - turns * PI_C
    odd = turns - 2.0 * jnp.floor(turns * 0.5)
    r = r * (1.0 - 2.0 * odd)
    r2 = r * r
    tail = -2.5052108e-8 + r2 * 1.6059044e-10
    tail = 2.7557319e-6 + r2 * tail
    tail = -1.9841270e-4 + r2 * tail
    tail = 8.3333333e-3 + r2 * tail
    tail = -1.6666667e-1 + r2 * tail
    return r + r * r2 * tail


def column(row):
    n = row.shape[1]
    square = jnp.broadcast_to(row, (n, n))
    at_row = lax.broadcasted_iota(jnp.int32, (n, n), 0)
    at_col = lax.broadcasted_iota(jnp.int32, (n, n), 1)
    return jnp.sum(jnp.where(at_row == at_col, square, 0.0), axis=1, keepdims=True)


def rows_to_rows(a, b):
    return lax.dot_general(
        a, b, (((0,), (0,)), ((), ())), precision=HIGHEST, preferred_element_type=F32
    )


def kernel(
    n,
    span,
    groups,
    size,
    q_hbm,
    k_hbm,
    v_hbm,
    taps_hbm,
    skip_hbm,
    freqs_hbm,
    phases_hbm,
    w1_hbm,
    b1_hbm,
    w2_hbm,
    b2_hbm,
    wo_hbm,
    rates_hbm,
    o_ref,
    taps_ref,
    skip_ref,
    freqs_ref,
    phases_ref,
    w1_ref,
    b1_ref,
    w2_ref,
    b2_ref,
    wo_ref,
    rates_ref,
    q_ref,
    k_ref,
    v_ref,
    halo_ref,
    ext_ref,
    sig_ref,
    xs_ref,
    xe_ref,
    xo_ref,
    hs_ref,
    ha_ref,
    f_ref,
    ys_ref,
    yr_ref,
    in_sem,
    small_sem,
    halo_send,
    halo_recv,
    x_send,
    x_recv,
    h_send,
    h_recv,
    y_send,
    y_recv,
):
    me = lax.axis_index("ctx")
    seq = span * n
    blocks = span // TB
    rows = size // 2
    part = blocks * rows
    pad = CHAIN * rows

    def peer(j):
        return lax.rem(me + j, n)

    def source(j):
        return lax.rem(me + (n - j), n)

    load_v = pltpu.make_async_copy(v_hbm, v_ref, in_sem.at[0])
    load_k = pltpu.make_async_copy(k_hbm, k_ref, in_sem.at[1])
    load_q = pltpu.make_async_copy(q_hbm, q_ref, in_sem.at[2])
    barrier = pltpu.get_barrier_semaphore()
    for j in range(1, n):
        pl.semaphore_signal(
            barrier, inc=1, device_id={"ctx": peer(j)}, device_id_type=MESH
        )
    load_v.start()
    load_k.start()
    loads = [
        pltpu.make_async_copy(src, dst, small_sem.at[i])
        for i, (src, dst) in enumerate(
            [
                (taps_hbm, taps_ref),
                (skip_hbm, skip_ref),
                (freqs_hbm, freqs_ref),
                (phases_hbm, phases_ref),
                (w1_hbm, w1_ref),
                (b1_hbm, b1_ref),
                (w2_hbm, w2_ref),
                (b2_hbm, b2_ref),
                (wo_hbm, wo_ref),
                (rates_hbm, rates_ref),
            ]
        )
    ]
    for load in loads:
        load.start()
    load_q.start()
    for h in range(2):
        xe_ref[h, 0:pad, :] = jnp.zeros((pad, TB), BF16)

    load_v.wait()
    pl.semaphore_wait(barrier, n - 1)
    halo = pltpu.make_async_remote_copy(
        src_ref=v_ref.at[pl.ds(span - 16, 16), :],
        dst_ref=halo_ref,
        send_sem=halo_send,
        recv_sem=halo_recv,
        device_id={"ctx": peer(1)},
        device_id_type=MESH,
    )
    halo.start()

    ext_ref[8:, :] = v_ref[...].astype(F32)
    loads[0].wait()
    load_k.wait()
    taps = taps_ref[...]

    def one_pair(i, _):
        turned = []
        for u in range(2):
            at = pl.multiple_of((2 * i + u) * TB, TB)
            mixed = taps[0:1] * ext_ref[pl.ds(at + 8, TB), :]
            mixed = mixed + taps[1:2] * ext_ref[pl.ds(at + 7, TB), :]
            mixed = mixed + taps[2:3] * ext_ref[pl.ds(at + 6, TB), :]
            signal = (k_ref[pl.ds(at, TB), :].astype(F32) * mixed).astype(BF16)
            sig_ref[pl.ds(at, TB), :] = signal
            turned.append(signal.astype(F32).T)
        for g in range(groups):
            for h in range(2):
                low = g * size + h * rows
                row = pl.multiple_of(h * part + i * size, size)
                xs_ref[g, pl.ds(row, size), :] = jnp.concatenate(
                    [turned[0][low : low + rows], turned[1][low : low + rows]], 0
                ).astype(BF16)
        return 0

    lax.fori_loop(1, blocks // 2, one_pair, 0)

    parts = [(0, size, part - size), (0, 0, size), (1, 0, part)]

    def x_copy(j, p):
        h, first, count = parts[p]
        at = pl.multiple_of(pad + me * part + first, 16)
        return pltpu.make_async_remote_copy(
            src_ref=xs_ref.at[peer(j), pl.ds(h * part + first, count), :],
            dst_ref=xe_ref.at[h, pl.ds(at, count), :],
            send_sem=x_send.at[p, j],
            recv_sem=x_recv.at[p, j],
            device_id={"ctx": peer(j)},
            device_id_type=MESH,
        )

    def x_wait(j, p):
        h, first, count = parts[p]
        at = pl.multiple_of(pad + source(j) * part + first, 16)
        pltpu.make_async_remote_copy(
            src_ref=xs_ref.at[peer(j), pl.ds(h * part + first, count), :],
            dst_ref=xe_ref.at[h, pl.ds(at, count), :],
            send_sem=x_send.at[p, j],
            recv_sem=x_recv.at[p, j],
            device_id={"ctx": peer(j)},
            device_id_type=MESH,
        ).wait()

    for j in range(1, n):
        x_copy(j, 0).start()

    for load in loads[1:]:
        load.wait()
    freq = column(freqs_ref[...]) * (2.0 * math.pi)
    phase = column(phases_ref[...])
    bias1 = column(b1_ref[...])
    bias2 = column(b2_ref[...])
    rate = column(rates_ref[...])
    wide = span

    def some_positions(i, _):
        start = me * span + i * wide
        lanes = lax.broadcasted_iota(jnp.int32, (1, wide), 1) + start
        scaled = lanes.astype(F32) / seq
        feature = sine(freq * scaled + phase)
        first = sine(rows_to_rows(w1_ref[...], feature) + bias1)
        second = sine(rows_to_rows(w2_ref[...], first) + bias2)
        values = lax.dot(
            wo_ref[...], second, precision=HIGHEST, preferred_element_type=F32
        ) * jnp.exp(-rate * scaled)
        for t in range(wide // 128):
            for g in range(groups):
                hs_ref[g, pl.ds(i * (wide // 128) + t, 1), :] = values[
                    g : g + 1, t * 128 : (t + 1) * 128
                ]
        return 0

    lax.fori_loop(0, span // wide, some_positions, 0)

    tiles = span // 128

    def h_copy(j):
        return pltpu.make_async_remote_copy(
            src_ref=hs_ref.at[peer(j)],
            dst_ref=ha_ref.at[pl.ds(pl.multiple_of(me * tiles, 8), tiles), :],
            send_sem=h_send.at[j],
            recv_sem=h_recv.at[j],
            device_id={"ctx": peer(j)},
            device_id_type=MESH,
        )

    halo.wait()
    ext_ref[0:8, :] = jnp.where(me > 0, halo_ref[8:16, :].astype(F32), 0.0)
    one_pair(0, 0)
    for j in range(1, n):
        x_copy(j, 1).start()
    for j in range(1, n):
        h_copy(j).start()
    for j in range(1, n):
        x_copy(j, 2).start()
    for h in range(2):
        at = pl.multiple_of(pad + me * part, 16)
        xe_ref[h, pl.ds(at, part), :] = xs_ref[me, h * part : (h + 1) * part, :]
    ha_ref[pl.ds(pl.multiple_of(me * tiles, 8), tiles), :] = hs_ref[me]
    for j in range(1, n):
        h_copy(j).wait()

    at_row = lax.broadcasted_iota(jnp.int32, (128, 128), 0)
    at_col = lax.broadcasted_iota(jnp.int32, (128, 128), 1)
    keep = at_col >= at_row
    f_ref[0] = jnp.zeros((128, 128), BF16)

    def one_tile(t, before):
        row = jnp.broadcast_to(ha_ref[pl.ds(t, 1), :], (128, 128))
        turned = pltpu.roll(row, 0, 1, stride=1, stride_axis=0)
        f_ref[t + 1] = jnp.where(keep, turned, before).astype(BF16)
        return turned

    lax.fori_loop(0, seq // 128, one_tile, jnp.zeros((128, 128), F32), unroll=32)

    def lag_block(lag):
        low, mid, high = f_ref[2 * lag], f_ref[2 * lag + 1], f_ref[2 * lag + 2]
        return jnp.concatenate(
            [jnp.concatenate([mid, high], 1), jnp.concatenate([low, mid], 1)], 0
        )

    def y_copy(h, to):
        j = lax.rem(to - me + n, n)
        return pltpu.make_async_remote_copy(
            src_ref=ys_ref.at[h, to],
            dst_ref=yr_ref.at[h, me],
            send_sem=y_send.at[h, j],
            recv_sem=y_recv.at[h, j],
            device_id={"ctx": to},
            device_id_type=MESH,
        )

    pairs = n // 2
    wide_rows = 2 * part
    for h in range(2):
        for p in range(3):
            if parts[p][0] == h:
                for j in range(1, n):
                    x_wait(j, p)
        whole = xe_ref[h].astype(F32)
        xo_ref[h] = jnp.concatenate(
            [jnp.zeros((rows, TB), F32), whole[: whole.shape[0] - rows]], 0
        ).astype(BF16)

        def one_pair_of_spans(k, _, h=h):
            two = lax.rem(me // 2 + 1 + k, pairs)
            for c in range(pairs):

                @pl.when(two == c)
                def _(c=c):
                    left, right = [], []
                    for lag in range((c + 1) * CHAIN):
                        start = pad + c * wide_rows - lag * rows
                        if start % 16 == 0:
                            left.append(xe_ref[h, start : start + wide_rows, :])
                        else:
                            start = start + rows
                            left.append(xo_ref[h, start : start + wide_rows, :])
                        right.append(lag_block(lag))
                    out = jnp.dot(
                        jnp.concatenate(left, 1),
                        jnp.concatenate(right, 0),
                        preferred_element_type=F32,
                    ).astype(BF16)
                    ys_ref[h, 2 * c] = out[:part]
                    ys_ref[h, 2 * c + 1] = out[part:]

            @pl.when(k < pairs - 1)
            def _():
                y_copy(h, 2 * two).start()
                y_copy(h, 2 * two + 1).start()

            return 0

        lax.fori_loop(0, pairs, one_pair_of_spans, 0)
        y_copy(h, me + 1 - 2 * lax.rem(me, 2)).start()
        yr_ref[h, me] = ys_ref[h, me]

    load_q.wait()
    for h in range(2):
        for j in range(1, n):
            pltpu.make_async_remote_copy(
                src_ref=ys_ref.at[h, peer(j)],
                dst_ref=yr_ref.at[h, source(j)],
                send_sem=y_send.at[h, j],
                recv_sem=y_recv.at[h, j],
                device_id={"ctx": peer(j)},
                device_id_type=MESH,
            ).wait()

    skip = skip_ref[...]

    def last_pair(i, _):
        row = pl.multiple_of(i * size, size)
        two = [
            yr_ref[h, g, pl.ds(row, size), :].astype(F32)
            for g in range(groups)
            for h in range(2)
        ]
        for u in range(2):
            at = pl.multiple_of((2 * i + u) * TB, TB)
            conv = jnp.concatenate([x[u * rows : (u + 1) * rows] for x in two], 0).T
            total = conv + skip * sig_ref[pl.ds(at, TB), :].astype(F32)
            o_ref[pl.ds(at, TB), :] = (
                q_ref[pl.ds(at, TB), :].astype(F32) * total
            ).astype(BF16)
        return 0

    lax.fori_loop(0, blocks // 2, last_pair, 0)


def on_device(
    q_feat,
    k_feat,
    v_feat,
    short_taps,
    skip_bias,
    freqs,
    phases,
    w_first,
    b_first,
    w_second,
    b_second,
    w_out,
    rates,
):
    n = lax.axis_size("ctx")
    span, channels = q_feat.shape
    groups = rates.shape[0]
    size = channels // groups
    seq = span * n
    blocks = span // TB
    piece = blocks * size
    part = piece // 2
    pad = CHAIN * size // 2
    hbm = pl.BlockSpec(memory_space=pltpu.HBM)
    vmem = pl.BlockSpec(memory_space=pltpu.VMEM)
    dma = pltpu.SemaphoreType.DMA
    return pl.pallas_call(
        functools.partial(kernel, n, span, groups, size),
        name="toeplitz_conv",
        out_shape=pltpu.VMEM((span, channels), BF16),
        in_specs=[hbm] * 13,
        out_specs=vmem,
        scratch_shapes=[
            pltpu.VMEM(short_taps.shape, F32),
            pltpu.VMEM((1, channels), F32),
            pltpu.VMEM((1, freqs.shape[0]), F32),
            pltpu.VMEM((1, phases.shape[0]), F32),
            pltpu.VMEM(w_first.shape, F32),
            pltpu.VMEM((1, b_first.shape[0]), F32),
            pltpu.VMEM(w_second.shape, F32),
            pltpu.VMEM((1, b_second.shape[0]), F32),
            pltpu.VMEM((groups, w_out.shape[0]), F32),
            pltpu.VMEM((1, groups), F32),
            pltpu.VMEM((span, channels), BF16),
            pltpu.VMEM((span, channels), BF16),
            pltpu.VMEM((span, channels), BF16),
            pltpu.VMEM((16, channels), BF16),
            pltpu.VMEM((span + 8, channels), F32),
            pltpu.VMEM((span, channels), BF16),
            pltpu.VMEM((groups, piece, TB), BF16),
            pltpu.VMEM((2, pad + n * part, TB), BF16),
            pltpu.VMEM((2, pad + n * part, TB), BF16),
            pltpu.VMEM((groups, span // 128, 128), F32),
            pltpu.VMEM((seq // 128, 128), F32),
            pltpu.VMEM((seq // 128 + 1, 128, 128), BF16),
            pltpu.VMEM((2, n, part, TB), BF16),
            pltpu.VMEM((2, groups, part, TB), BF16),
            dma((3,)),
            dma((10,)),
            dma,
            dma,
            dma((3, n)),
            dma((3, n)),
            dma((n,)),
            dma((n,)),
            dma((2, n)),
            dma((2, n)),
        ],
        compiler_params=pltpu.CompilerParams(
            collective_id=0, has_side_effects=True, vmem_limit_bytes=62 << 20
        ),
    )(
        q_feat,
        k_feat,
        v_feat,
        short_taps,
        skip_bias.reshape(1, -1),
        freqs.reshape(1, -1),
        phases.reshape(1, -1),
        w_first,
        b_first.reshape(1, -1),
        w_second,
        b_second.reshape(1, -1),
        w_out.T,
        rates.reshape(1, -1),
    )


def solution(mesh):
    return jax.shard_map(
        on_device,
        mesh=mesh,
        in_specs=(
            P("ctx", "dp"),
            P("ctx", "dp"),
            P("ctx", "dp"),
            P(None, "dp"),
            P("dp"),
            P(),
            P(),
            P(),
            P(),
            P(),
            P(),
            P(None, "dp"),
            P("dp"),
        ),
        out_specs=P("ctx", "dp"),
        check_vma=False,
    )
```

```python
import functools
import math

import jax
import jax.numpy as jnp
from jax import lax
from jax.experimental import pallas as pl
from jax.experimental.pallas import tpu as pltpu
from jax.sharding import PartitionSpec as P

MESH = pl.DeviceIdType.MESH
F32 = jnp.float32
BF16 = jnp.bfloat16
HIGHEST = lax.Precision.HIGHEST

TB = 256
CHAIN = 16
FAR = ((1, 2), (1, 1), (1, 3), (0, 2), (1, 0), (0, 1), (0, 3))

PI_A = 3.140625
PI_B = 9.67025756835938e-04
PI_C = 6.277114152908325e-07


def sine(x):
    turns = jnp.floor(x * (1.0 / math.pi) + 0.5)
    r = ((x - turns * PI_A) - turns * PI_B) - turns * PI_C
    odd = turns - 2.0 * jnp.floor(turns * 0.5)
    r = r * (1.0 - 2.0 * odd)
    r2 = r * r
    tail = -2.5052108e-8 + r2 * 1.6059044e-10
    tail = 2.7557319e-6 + r2 * tail
    tail = -1.9841270e-4 + r2 * tail
    tail = 8.3333333e-3 + r2 * tail
    tail = -1.6666667e-1 + r2 * tail
    return r + r * r2 * tail


def column(row):
    n = row.shape[1]
    square = jnp.broadcast_to(row, (n, n))
    at_row = lax.broadcasted_iota(jnp.int32, (n, n), 0)
    at_col = lax.broadcasted_iota(jnp.int32, (n, n), 1)
    return jnp.sum(jnp.where(at_row == at_col, square, 0.0), axis=1, keepdims=True)


def rows_to_rows(a, b):
    return lax.dot_general(
        a, b, (((0,), (0,)), ((), ())), precision=HIGHEST, preferred_element_type=F32
    )


def kernel(
    n,
    span,
    groups,
    size,
    q_hbm,
    k_hbm,
    v_hbm,
    taps_hbm,
    skip_hbm,
    freqs_hbm,
    phases_hbm,
    w1_hbm,
    b1_hbm,
    w2_hbm,
    b2_hbm,
    wo_hbm,
    rates_hbm,
    o_ref,
    taps_ref,
    skip_ref,
    freqs_ref,
    phases_ref,
    w1_ref,
    b1_ref,
    w2_ref,
    b2_ref,
    wo_ref,
    rates_ref,
    q_ref,
    k_ref,
    v_ref,
    halo_ref,
    ext_ref,
    sig_ref,
    xs_ref,
    xe_ref,
    xo_ref,
    hs_ref,
    ha_ref,
    f_ref,
    ys_ref,
    yr_ref,
    in_sem,
    small_sem,
    halo_send,
    halo_recv,
    x_send,
    x_recv,
    h_send,
    h_recv,
    y_send,
    y_recv,
):
    me = lax.axis_index("ctx")
    seq = span * n
    blocks = span // TB
    rows = size // 2
    part = blocks * rows
    pad = CHAIN * rows

    side, place = me // 4, lax.rem(me, 4)

    def peer(step):
        return lax.rem(side + step[0], 2) * 4 + lax.rem(place + step[1], 4)

    def source(step):
        return lax.rem(side + step[0], 2) * 4 + lax.rem(place + 4 - step[1], 4)

    def slot(step):
        return step[0] * 4 + step[1]

    load_v = pltpu.make_async_copy(v_hbm, v_ref, in_sem.at[0])
    load_k = pltpu.make_async_copy(k_hbm, k_ref, in_sem.at[1])
    load_q = pltpu.make_async_copy(q_hbm, q_ref, in_sem.at[2])
    barrier = pltpu.get_barrier_semaphore()
    for step in FAR:
        pl.semaphore_signal(
            barrier, inc=1, device_id={"ctx": peer(step)}, device_id_type=MESH
        )
    load_v.start()
    load_k.start()
    loads = [
        pltpu.make_async_copy(src, dst, small_sem.at[i])
        for i, (src, dst) in enumerate(
            [
                (taps_hbm, taps_ref),
                (skip_hbm, skip_ref),
                (freqs_hbm, freqs_ref),
                (phases_hbm, phases_ref),
                (w1_hbm, w1_ref),
                (b1_hbm, b1_ref),
                (w2_hbm, w2_ref),
                (b2_hbm, b2_ref),
                (wo_hbm, wo_ref),
                (rates_hbm, rates_ref),
            ]
        )
    ]
    for load in loads:
        load.start()
    load_q.start()
    for h in range(2):
        xe_ref[h, 0:pad, :] = jnp.zeros((pad, TB), BF16)

    load_v.wait()
    pl.semaphore_wait(barrier, n - 1)
    halo = pltpu.make_async_remote_copy(
        src_ref=v_ref.at[pl.ds(span - 16, 16), :],
        dst_ref=halo_ref,
        send_sem=halo_send,
        recv_sem=halo_recv,
        device_id={"ctx": lax.rem(me + 1, n)},
        device_id_type=MESH,
    )
    halo.start()

    ext_ref[8:, :] = v_ref[...].astype(F32)
    for load in loads:
        load.wait()
    load_k.wait()
    taps = taps_ref[...]

    def one_pair(i, _):
        turned = []
        for u in range(2):
            at = pl.multiple_of((2 * i + u) * TB, TB)
            mixed = taps[0:1] * ext_ref[pl.ds(at + 8, TB), :]
            mixed = mixed + taps[1:2] * ext_ref[pl.ds(at + 7, TB), :]
            mixed = mixed + taps[2:3] * ext_ref[pl.ds(at + 6, TB), :]
            signal = (k_ref[pl.ds(at, TB), :].astype(F32) * mixed).astype(BF16)
            sig_ref[pl.ds(at, TB), :] = signal
            turned.append(signal.astype(F32).T)
        for g in range(groups):
            for h in range(2):
                low = g * size + h * rows
                row = pl.multiple_of(h * part + i * size, size)
                xs_ref[g, pl.ds(row, size), :] = jnp.concatenate(
                    [turned[0][low : low + rows], turned[1][low : low + rows]], 0
                ).astype(BF16)
        return 0

    for i in range(1, blocks // 2):
        one_pair(i, 0)

    parts = [(0, size, part - size), (0, 0, size), (1, 0, part)]

    def x_copy(step, p):
        h, first, count = parts[p]
        at = pl.multiple_of(pad + me * part + first, 16)
        return pltpu.make_async_remote_copy(
            src_ref=xs_ref.at[peer(step), pl.ds(h * part + first, count), :],
            dst_ref=xe_ref.at[h, pl.ds(at, count), :],
            send_sem=x_send.at[p, slot(step)],
            recv_sem=x_recv.at[p, slot(step)],
            device_id={"ctx": peer(step)},
            device_id_type=MESH,
        )

    def x_wait(step, p):
        h, first, count = parts[p]
        at = pl.multiple_of(pad + source(step) * part + first, 16)
        pltpu.make_async_remote_copy(
            src_ref=xs_ref.at[peer(step), pl.ds(h * part + first, count), :],
            dst_ref=xe_ref.at[h, pl.ds(at, count), :],
            send_sem=x_send.at[p, slot(step)],
            recv_sem=x_recv.at[p, slot(step)],
            device_id={"ctx": peer(step)},
            device_id_type=MESH,
        ).wait()

    for step in FAR:
        x_copy(step, 0).start()

    freq = column(freqs_ref[...]) * (2.0 * math.pi)
    phase = column(phases_ref[...])
    bias1 = column(b1_ref[...])
    bias2 = column(b2_ref[...])
    rate = column(rates_ref[...])
    wide = span

    def some_positions(i):
        start = me * span + i * wide
        lanes = lax.broadcasted_iota(jnp.int32, (1, wide), 1) + start
        scaled = lanes.astype(F32) / seq
        feature = sine(freq * scaled + phase)
        first = sine(rows_to_rows(w1_ref[...], feature) + bias1)
        second = sine(rows_to_rows(w2_ref[...], first) + bias2)
        values = lax.dot(
            wo_ref[...], second, precision=HIGHEST, preferred_element_type=F32
        ) * jnp.exp(-rate * scaled)
        for t in range(wide // 128):
            for g in range(groups):
                hs_ref[g, pl.ds(i * (wide // 128) + t, 1), :] = values[
                    g : g + 1, t * 128 : (t + 1) * 128
                ]

    for i in range(span // wide):
        some_positions(i)

    tiles = span // 128

    def h_copy(step):
        return pltpu.make_async_remote_copy(
            src_ref=hs_ref.at[peer(step)],
            dst_ref=ha_ref.at[pl.ds(pl.multiple_of(me * tiles, 8), tiles), :],
            send_sem=h_send.at[slot(step)],
            recv_sem=h_recv.at[slot(step)],
            device_id={"ctx": peer(step)},
            device_id_type=MESH,
        )

    for step in FAR:
        h_copy(step).start()
    def h_wait(step):
        at = pl.multiple_of(source(step) * tiles, 8)
        pltpu.make_async_remote_copy(
            src_ref=hs_ref.at[peer(step)],
            dst_ref=ha_ref.at[pl.ds(at, tiles), :],
            send_sem=h_send.at[slot(step)],
            recv_sem=h_recv.at[slot(step)],
            device_id={"ctx": peer(step)},
            device_id_type=MESH,
        ).wait()

    halo.wait()
    ext_ref[0:8, :] = jnp.where(me > 0, halo_ref[8:16, :].astype(F32), 0.0)
    one_pair(0, 0)
    for step in FAR:
        x_copy(step, 1).start()
    for step in FAR:
        x_copy(step, 2).start()
    for h in range(2):
        at = pl.multiple_of(pad + me * part, 16)
        xe_ref[h, pl.ds(at, part), :] = xs_ref[me, h * part : (h + 1) * part, :]
    ha_ref[pl.ds(pl.multiple_of(me * tiles, 8), tiles), :] = hs_ref[me]

    at_row = lax.broadcasted_iota(jnp.int32, (128, 128), 0)
    at_col = lax.broadcasted_iota(jnp.int32, (128, 128), 1)
    keep = at_col >= at_row
    f_ref[0] = jnp.zeros((128, 128), BF16)

    def turned_row(at):
        row = jnp.broadcast_to(ha_ref[pl.ds(at, 1), :], (128, 128))
        return pltpu.roll(row, 0, 1, stride=1, stride_axis=0)

    for step in ((0, 0),) + FAR[::-1]:
        if step != (0, 0):
            h_wait(step)
        first = source(step) * tiles
        before = turned_row(first)
        for i in range(1, tiles):
            here = turned_row(first + i)
            f_ref[first + i + 1] = jnp.where(keep, here, before).astype(BF16)
            before = here
    for s in range(n):
        here = turned_row(s * tiles)
        if s == 0:
            before = jnp.zeros((128, 128), F32)
        else:
            before = turned_row(s * tiles - 1)
        f_ref[s * tiles + 1] = jnp.where(keep, here, before).astype(BF16)

    def lag_block(lag):
        low, mid, high = f_ref[2 * lag], f_ref[2 * lag + 1], f_ref[2 * lag + 2]
        return jnp.concatenate(
            [jnp.concatenate([mid, high], 1), jnp.concatenate([low, mid], 1)], 0
        )

    halves = [(0, part), (part, part), (0, 2 * part)]

    def y_copy(kind, to, other, index):
        first, count = halves[kind]
        return pltpu.make_async_remote_copy(
            src_ref=ys_ref.at[to, pl.ds(first, count), :],
            dst_ref=yr_ref.at[other, pl.ds(first, count), :],
            send_sem=y_send.at[kind, index],
            recv_sem=y_recv.at[kind, index],
            device_id={"ctx": to},
            device_id_type=MESH,
        )

    def shifted(h, start, count):
        if start % 16 == 0:
            return xe_ref[h, start : start + count, :]
        return xo_ref[h, start + rows : start + rows + count, :]

    def chain(halves_of, first, count, lags):
        left = [
            jnp.concatenate(
                [shifted(h, pad + first - lag * rows, count) for h in halves_of], 0
            )
            for lag in range(lags)
        ]
        right = [lag_block(lag) for lag in range(lags)]
        return jnp.dot(
            jnp.concatenate(left, 1),
            jnp.concatenate(right, 0),
            preferred_element_type=F32,
        ).astype(BF16)

    for h in range(2):
        for p in range(3):
            if parts[p][0] == h:
                for step in FAR[::-1]:
                    x_wait(step, p)
        whole = xe_ref[h].astype(F32)
        xo_ref[h] = jnp.concatenate(
            [jnp.zeros((rows, TB), F32), whole[: whole.shape[0] - rows]], 0
        ).astype(BF16)

        for other in range(2):

            @pl.when(side == 1 - other)
            def _(other=other, h=h):
                for c in (4 * other + 2, 4 * other):
                    out = chain((h,), c * part, 2 * part, (c + 2) * blocks)
                    ys_ref[c, h * part : (h + 1) * part] = out[:part]
                    ys_ref[c + 1, h * part : (h + 1) * part] = out[part:]

        for move in (2, 1, 3, 0):
            y_copy(h, peer((1, move)), me, move).start()

    def one_span(i, _):
        move = (1 - i // 2) * (2 + i) + (i // 2) * (3 - i)
        to = side * 4 + lax.rem(place + move, 4)
        for c in range(n):

            @pl.when(to == c)
            def _(c=c):
                ys_ref[c] = chain((0, 1), c * part, part, (c + 1) * blocks)

        @pl.when(i < 3)
        def _():
            y_copy(2, to, me, move).start()

        return 0

    lax.fori_loop(0, 4, one_span, 0)
    yr_ref[me] = ys_ref[me]

    load_q.wait()
    for step in FAR:
        for kind in (0, 1) if step[0] else (2,):
            first, count = halves[kind]
            pltpu.make_async_remote_copy(
                src_ref=ys_ref.at[peer(step), pl.ds(first, count), :],
                dst_ref=yr_ref.at[source(step), pl.ds(first, count), :],
                send_sem=y_send.at[kind, step[1]],
                recv_sem=y_recv.at[kind, step[1]],
                device_id={"ctx": peer(step)},
                device_id_type=MESH,
            ).wait()

    skip = skip_ref[...]

    def last_pair(i, _):
        row = pl.multiple_of(i * size, size)
        two = [
            yr_ref[g, pl.ds(pl.multiple_of(h * part + row, 16), size), :].astype(F32)
            for g in range(groups)
            for h in range(2)
        ]
        for u in range(2):
            at = pl.multiple_of((2 * i + u) * TB, TB)
            conv = jnp.concatenate([x[u * rows : (u + 1) * rows] for x in two], 0).T
            total = conv + skip * sig_ref[pl.ds(at, TB), :].astype(F32)
            o_ref[pl.ds(at, TB), :] = (
                q_ref[pl.ds(at, TB), :].astype(F32) * total
            ).astype(BF16)
        return 0

    lax.fori_loop(0, blocks // 2, last_pair, 0)


def on_device(
    q_feat,
    k_feat,
    v_feat,
    short_taps,
    skip_bias,
    freqs,
    phases,
    w_first,
    b_first,
    w_second,
    b_second,
    w_out,
    rates,
):
    n = lax.axis_size("ctx")
    span, channels = q_feat.shape
    groups = rates.shape[0]
    size = channels // groups
    seq = span * n
    blocks = span // TB
    piece = blocks * size
    part = piece // 2
    pad = CHAIN * size // 2
    hbm = pl.BlockSpec(memory_space=pltpu.HBM)
    vmem = pl.BlockSpec(memory_space=pltpu.VMEM)
    dma = pltpu.SemaphoreType.DMA
    return pl.pallas_call(
        functools.partial(kernel, n, span, groups, size),
        name="toeplitz_conv",
        out_shape=pltpu.VMEM((span, channels), BF16),
        in_specs=[hbm] * 13,
        out_specs=vmem,
        scratch_shapes=[
            pltpu.VMEM(short_taps.shape, F32),
            pltpu.VMEM((1, channels), F32),
            pltpu.VMEM((1, freqs.shape[0]), F32),
            pltpu.VMEM((1, phases.shape[0]), F32),
            pltpu.VMEM(w_first.shape, F32),
            pltpu.VMEM((1, b_first.shape[0]), F32),
            pltpu.VMEM(w_second.shape, F32),
            pltpu.VMEM((1, b_second.shape[0]), F32),
            pltpu.VMEM((groups, w_out.shape[0]), F32),
            pltpu.VMEM((1, groups), F32),
            pltpu.VMEM((span, channels), BF16),
            pltpu.VMEM((span, channels), BF16),
            pltpu.VMEM((span, channels), BF16),
            pltpu.VMEM((16, channels), BF16),
            pltpu.VMEM((span + 8, channels), F32),
            pltpu.VMEM((span, channels), BF16),
            pltpu.VMEM((groups, piece, TB), BF16),
            pltpu.VMEM((2, pad + n * part, TB), BF16),
            pltpu.VMEM((2, pad + n * part, TB), BF16),
            pltpu.VMEM((groups, span // 128, 128), F32),
            pltpu.VMEM((seq // 128, 128), F32),
            pltpu.VMEM((seq // 128 + 1, 128, 128), BF16),
            pltpu.VMEM((n, piece, TB), BF16),
            pltpu.VMEM((groups, piece, TB), BF16),
            dma((3,)),
            dma((10,)),
            dma,
            dma,
            dma((3, n)),
            dma((3, n)),
            dma((n,)),
            dma((n,)),
            dma((3, 4)),
            dma((3, 4)),
        ],
        compiler_params=pltpu.CompilerParams(
            collective_id=0, has_side_effects=True, vmem_limit_bytes=62 << 20
        ),
    )(
        q_feat,
        k_feat,
        v_feat,
        short_taps,
        skip_bias.reshape(1, -1),
        freqs.reshape(1, -1),
        phases.reshape(1, -1),
        w_first,
        b_first.reshape(1, -1),
        w_second,
        b_second.reshape(1, -1),
        w_out.T,
        rates.reshape(1, -1),
    )


def solution(mesh):
    return jax.shard_map(
        on_device,
        mesh=mesh,
        in_specs=(
            P("ctx", "dp"),
            P("ctx", "dp"),
            P("ctx", "dp"),
            P(None, "dp"),
            P("dp"),
            P(),
            P(),
            P(),
            P(),
            P(),
            P(),
            P(None, "dp"),
            P("dp"),
        ),
        out_specs=P("ctx", "dp"),
        check_vma=False,
    )
```

```python
import functools
import math

import jax
import jax.numpy as jnp
from jax import lax
from jax.experimental import pallas as pl
from jax.experimental.pallas import tpu as pltpu
from jax.sharding import PartitionSpec as P

MESH = pl.DeviceIdType.MESH
F32 = jnp.float32
BF16 = jnp.bfloat16

TB = 256
CHAIN = 16
FAR = ((1, 2), (1, 1), (1, 3), (0, 2), (1, 0), (0, 1), (0, 3))

TURN_A = 6.28125
TURN_B = 0.001934051513671875
TURN_C = 1.2556658930407139e-06
TURN_BC = 0.0019353071693331003


def sine(x, small=False):
    turns = jnp.round(x * (0.5 / math.pi))
    r = x - turns * TURN_A
    if small:
        r = r - turns * TURN_BC
    else:
        r = (r - turns * TURN_B) - turns * TURN_C
    r2 = r * r
    tail = -2.4676328536088477e-08 + r2 * 1.3449288904787693e-10
    tail = 2.7529381441127043e-06 + r2 * tail
    tail = -0.00019840151071548462 + r2 * tail
    tail = 0.00833331048488617 + r2 * tail
    tail = -0.166666641831398 + r2 * tail
    return r + r * (r2 * tail)


def column(row):
    n = row.shape[1]
    square = jnp.broadcast_to(row, (n, n))
    at_row = lax.broadcasted_iota(jnp.int32, (n, n), 0)
    at_col = lax.broadcasted_iota(jnp.int32, (n, n), 1)
    return jnp.sum(jnp.where(at_row == at_col, square, 0.0), axis=1, keepdims=True)


def high_low(value):
    high = value.astype(BF16)
    return high, (value - high.astype(F32)).astype(BF16)


def stacked(weights):
    high, low = high_low(weights)
    return jnp.concatenate([high, high, low], 1)


def product(stack, value):
    high, low = high_low(value)
    return jnp.dot(
        stack, jnp.concatenate([high, low, high], 0), preferred_element_type=F32
    )


def kernel(
    n,
    span,
    groups,
    size,
    q_hbm,
    k_hbm,
    v_hbm,
    taps_hbm,
    skip_hbm,
    freqs_hbm,
    phases_hbm,
    w1_hbm,
    b1_hbm,
    w2_hbm,
    b2_hbm,
    wo_hbm,
    rates_hbm,
    o_ref,
    taps_ref,
    skip_ref,
    freqs_ref,
    phases_ref,
    w1_ref,
    b1_ref,
    w2_ref,
    b2_ref,
    wo_ref,
    rates_ref,
    q_ref,
    k_ref,
    v_ref,
    halo_ref,
    ext_ref,
    sig_ref,
    xs_ref,
    xe_ref,
    xo_ref,
    hs_ref,
    ha_ref,
    f_ref,
    ys_ref,
    yr_ref,
    in_sem,
    small_sem,
    halo_send,
    halo_recv,
    x_send,
    x_recv,
    h_send,
    h_recv,
    y_send,
    y_recv,
):
    me = lax.axis_index("ctx")
    seq = span * n
    blocks = span // TB
    rows = size // 2
    part = blocks * rows
    pad = CHAIN * rows

    side, place = me // 4, lax.rem(me, 4)

    def peer(step):
        return lax.rem(side + step[0], 2) * 4 + lax.rem(place + step[1], 4)

    def source(step):
        return lax.rem(side + step[0], 2) * 4 + lax.rem(place + 4 - step[1], 4)

    def slot(step):
        return step[0] * 4 + step[1]

    load_v = pltpu.make_async_copy(v_hbm, v_ref, in_sem.at[0])
    load_k = pltpu.make_async_copy(k_hbm, k_ref, in_sem.at[1])
    load_q = pltpu.make_async_copy(q_hbm, q_ref, in_sem.at[2])
    barrier = pltpu.get_barrier_semaphore()
    for step in FAR:
        pl.semaphore_signal(
            barrier, inc=1, device_id={"ctx": peer(step)}, device_id_type=MESH
        )
    load_v.start()
    load_k.start()
    loads = [
        pltpu.make_async_copy(src, dst, small_sem.at[i])
        for i, (src, dst) in enumerate(
            [
                (taps_hbm, taps_ref),
                (skip_hbm, skip_ref),
                (freqs_hbm, freqs_ref),
                (phases_hbm, phases_ref),
                (w1_hbm, w1_ref),
                (b1_hbm, b1_ref),
                (w2_hbm, w2_ref),
                (b2_hbm, b2_ref),
                (wo_hbm, wo_ref),
                (rates_hbm, rates_ref),
            ]
        )
    ]
    for load in loads:
        load.start()
    load_q.start()
    for h in range(2):
        xe_ref[h, 0:pad, :] = jnp.zeros((pad, TB), BF16)

    load_v.wait()
    pl.semaphore_wait(barrier, n - 1)
    halo = pltpu.make_async_remote_copy(
        src_ref=v_ref.at[pl.ds(span - 16, 16), :],
        dst_ref=halo_ref,
        send_sem=halo_send,
        recv_sem=halo_recv,
        device_id={"ctx": lax.rem(me + 1, n)},
        device_id_type=MESH,
    )
    halo.start()

    ext_ref[8:, :] = v_ref[...].astype(F32)
    for load in loads:
        load.wait()
    load_k.wait()
    taps = taps_ref[...]

    def one_pair(i, _):
        turned = []
        for u in range(2):
            at = pl.multiple_of((2 * i + u) * TB, TB)
            mixed = taps[0:1] * ext_ref[pl.ds(at + 8, TB), :]
            mixed = mixed + taps[1:2] * ext_ref[pl.ds(at + 7, TB), :]
            mixed = mixed + taps[2:3] * ext_ref[pl.ds(at + 6, TB), :]
            signal = (k_ref[pl.ds(at, TB), :].astype(F32) * mixed).astype(BF16)
            sig_ref[pl.ds(at, TB), :] = signal
            turned.append(signal.astype(F32).T)
        for g in range(groups):
            for h in range(2):
                low = g * size + h * rows
                row = pl.multiple_of(h * part + i * size, size)
                xs_ref[g, pl.ds(row, size), :] = jnp.concatenate(
                    [turned[0][low : low + rows], turned[1][low : low + rows]], 0
                ).astype(BF16)
        return 0

    for i in range(1, blocks // 2):
        one_pair(i, 0)

    parts = [(0, size, part - size), (0, 0, size), (1, 0, part)]

    def x_copy(step, p):
        h, first, count = parts[p]
        at = pl.multiple_of(pad + me * part + first, 16)
        return pltpu.make_async_remote_copy(
            src_ref=xs_ref.at[peer(step), pl.ds(h * part + first, count), :],
            dst_ref=xe_ref.at[h, pl.ds(at, count), :],
            send_sem=x_send.at[p, slot(step)],
            recv_sem=x_recv.at[p, slot(step)],
            device_id={"ctx": peer(step)},
            device_id_type=MESH,
        )

    def x_wait(step, p):
        h, first, count = parts[p]
        at = pl.multiple_of(pad + source(step) * part + first, 16)
        pltpu.make_async_remote_copy(
            src_ref=xs_ref.at[peer(step), pl.ds(h * part + first, count), :],
            dst_ref=xe_ref.at[h, pl.ds(at, count), :],
            send_sem=x_send.at[p, slot(step)],
            recv_sem=x_recv.at[p, slot(step)],
            device_id={"ctx": peer(step)},
            device_id_type=MESH,
        ).wait()

    for step in FAR:
        x_copy(step, 0).start()

    freq = column(freqs_ref[...]) * (2.0 * math.pi)
    phase = column(phases_ref[...])
    bias1 = column(b1_ref[...])
    bias2 = column(b2_ref[...])
    rate = column(rates_ref[...])
    layer1 = stacked(w1_ref[...].T)
    layer2 = stacked(w2_ref[...].T)
    layer3 = stacked(wo_ref[...])

    wide = span

    def some_positions(i):
        start = me * span + i * wide
        lanes = lax.broadcasted_iota(jnp.int32, (1, wide), 1) + start
        scaled = lanes.astype(F32) / seq
        feature = sine(freq * scaled + phase)
        first = sine(product(layer1, feature) + bias1, small=True)
        second = sine(product(layer2, first) + bias2, small=True)
        values = product(layer3, second) * jnp.exp(-rate * scaled)
        for t in range(wide // 128):
            for g in range(groups):
                hs_ref[g, pl.ds(i * (wide // 128) + t, 1), :] = values[
                    g : g + 1, t * 128 : (t + 1) * 128
                ]

    for i in range(span // wide):
        some_positions(i)

    tiles = span // 128

    def h_copy(step):
        return pltpu.make_async_remote_copy(
            src_ref=hs_ref.at[peer(step)],
            dst_ref=ha_ref.at[pl.ds(pl.multiple_of(me * tiles, 8), tiles), :],
            send_sem=h_send.at[slot(step)],
            recv_sem=h_recv.at[slot(step)],
            device_id={"ctx": peer(step)},
            device_id_type=MESH,
        )

    for step in FAR:
        h_copy(step).start()
    def h_wait(step):
        at = pl.multiple_of(source(step) * tiles, 8)
        pltpu.make_async_remote_copy(
            src_ref=hs_ref.at[peer(step)],
            dst_ref=ha_ref.at[pl.ds(at, tiles), :],
            send_sem=h_send.at[slot(step)],
            recv_sem=h_recv.at[slot(step)],
            device_id={"ctx": peer(step)},
            device_id_type=MESH,
        ).wait()

    halo.wait()
    ext_ref[0:8, :] = jnp.where(me > 0, halo_ref[8:16, :].astype(F32), 0.0)
    one_pair(0, 0)
    for step in FAR:
        x_copy(step, 1).start()
    for step in FAR:
        x_copy(step, 2).start()
    for h in range(2):
        at = pl.multiple_of(pad + me * part, 16)
        xe_ref[h, pl.ds(at, part), :] = xs_ref[me, h * part : (h + 1) * part, :]
    ha_ref[pl.ds(pl.multiple_of(me * tiles, 8), tiles), :] = hs_ref[me]

    at_row = lax.broadcasted_iota(jnp.int32, (128, 128), 0)
    at_col = lax.broadcasted_iota(jnp.int32, (128, 128), 1)
    keep = at_col >= at_row
    f_ref[0] = jnp.zeros((128, 128), BF16)

    def turned_row(at):
        row = jnp.broadcast_to(ha_ref[pl.ds(at, 1), :], (128, 128))
        return pltpu.roll(row, 0, 1, stride=1, stride_axis=0)

    for step in ((0, 0),) + FAR[::-1]:
        if step != (0, 0):
            h_wait(step)
        first = source(step) * tiles
        before = turned_row(first)
        for i in range(1, tiles):
            here = turned_row(first + i)
            f_ref[first + i + 1] = jnp.where(keep, here, before).astype(BF16)
            before = here
    for s in range(n):
        here = turned_row(s * tiles)
        if s == 0:
            before = jnp.zeros((128, 128), F32)
        else:
            before = turned_row(s * tiles - 1)
        f_ref[s * tiles + 1] = jnp.where(keep, here, before).astype(BF16)

    def lag_block(lag):
        low, mid, high = f_ref[2 * lag], f_ref[2 * lag + 1], f_ref[2 * lag + 2]
        return jnp.concatenate(
            [jnp.concatenate([mid, high], 1), jnp.concatenate([low, mid], 1)], 0
        )

    halves = [(0, part), (part, part), (0, 2 * part)]

    def y_copy(kind, to, other, index):
        first, count = halves[kind]
        return pltpu.make_async_remote_copy(
            src_ref=ys_ref.at[to, pl.ds(first, count), :],
            dst_ref=yr_ref.at[other, pl.ds(first, count), :],
            send_sem=y_send.at[kind, index],
            recv_sem=y_recv.at[kind, index],
            device_id={"ctx": to},
            device_id_type=MESH,
        )

    def shifted(h, start, count):
        if start % 16 == 0:
            return xe_ref[h, start : start + count, :]
        return xo_ref[h, start + rows : start + rows + count, :]

    def chain(halves_of, first, count, lags):
        left = [
            jnp.concatenate(
                [shifted(h, pad + first - lag * rows, count) for h in halves_of], 0
            )
            for lag in range(lags)
        ]
        right = [lag_block(lag) for lag in range(lags)]
        return jnp.dot(
            jnp.concatenate(left, 1),
            jnp.concatenate(right, 0),
            preferred_element_type=F32,
        ).astype(BF16)

    for h in range(2):
        for p in range(3):
            if parts[p][0] == h:
                for step in FAR[::-1]:
                    x_wait(step, p)
        whole = xe_ref[h].astype(F32)
        xo_ref[h] = jnp.concatenate(
            [jnp.zeros((rows, TB), F32), whole[: whole.shape[0] - rows]], 0
        ).astype(BF16)

        for other in range(2):

            @pl.when(side == 1 - other)
            def _(other=other, h=h):
                for c in (4 * other + 2, 4 * other):
                    out = chain((h,), c * part, 2 * part, (c + 2) * blocks)
                    ys_ref[c, h * part : (h + 1) * part] = out[:part]
                    ys_ref[c + 1, h * part : (h + 1) * part] = out[part:]

        for move in (2, 1, 3, 0):
            y_copy(h, peer((1, move)), me, move).start()

    def one_span(i, _):
        move = (1 - i // 2) * (2 + i) + (i // 2) * (3 - i)
        to = side * 4 + lax.rem(place + move, 4)
        for c in range(n):

            @pl.when(to == c)
            def _(c=c):
                ys_ref[c] = chain((0, 1), c * part, part, (c + 1) * blocks)

        @pl.when(i < 3)
        def _():
            y_copy(2, to, me, move).start()

        return 0

    lax.fori_loop(0, 4, one_span, 0)
    yr_ref[me] = ys_ref[me]

    load_q.wait()
    for step in FAR:
        for kind in (0, 1) if step[0] else (2,):
            first, count = halves[kind]
            pltpu.make_async_remote_copy(
                src_ref=ys_ref.at[peer(step), pl.ds(first, count), :],
                dst_ref=yr_ref.at[source(step), pl.ds(first, count), :],
                send_sem=y_send.at[kind, step[1]],
                recv_sem=y_recv.at[kind, step[1]],
                device_id={"ctx": peer(step)},
                device_id_type=MESH,
            ).wait()

    skip = skip_ref[...]

    def last_pair(i, _):
        row = pl.multiple_of(i * size, size)
        two = [
            yr_ref[g, pl.ds(pl.multiple_of(h * part + row, 16), size), :].astype(F32)
            for g in range(groups)
            for h in range(2)
        ]
        for u in range(2):
            at = pl.multiple_of((2 * i + u) * TB, TB)
            conv = jnp.concatenate([x[u * rows : (u + 1) * rows] for x in two], 0).T
            total = conv + skip * sig_ref[pl.ds(at, TB), :].astype(F32)
            o_ref[pl.ds(at, TB), :] = (
                q_ref[pl.ds(at, TB), :].astype(F32) * total
            ).astype(BF16)
        return 0

    for i in range(blocks // 2):
        last_pair(i, 0)


def on_device(
    q_feat,
    k_feat,
    v_feat,
    short_taps,
    skip_bias,
    freqs,
    phases,
    w_first,
    b_first,
    w_second,
    b_second,
    w_out,
    rates,
):
    n = lax.axis_size("ctx")
    span, channels = q_feat.shape
    groups = rates.shape[0]
    size = channels // groups
    seq = span * n
    blocks = span // TB
    piece = blocks * size
    part = piece // 2
    pad = CHAIN * size // 2
    hbm = pl.BlockSpec(memory_space=pltpu.HBM)
    vmem = pl.BlockSpec(memory_space=pltpu.VMEM)
    dma = pltpu.SemaphoreType.DMA
    return pl.pallas_call(
        functools.partial(kernel, n, span, groups, size),
        name="toeplitz_conv",
        out_shape=pltpu.VMEM((span, channels), BF16),
        in_specs=[hbm] * 13,
        out_specs=vmem,
        scratch_shapes=[
            pltpu.VMEM(short_taps.shape, F32),
            pltpu.VMEM((1, channels), F32),
            pltpu.VMEM((1, freqs.shape[0]), F32),
            pltpu.VMEM((1, phases.shape[0]), F32),
            pltpu.VMEM(w_first.shape, F32),
            pltpu.VMEM((1, b_first.shape[0]), F32),
            pltpu.VMEM(w_second.shape, F32),
            pltpu.VMEM((1, b_second.shape[0]), F32),
            pltpu.VMEM((groups, w_out.shape[0]), F32),
            pltpu.VMEM((1, groups), F32),
            pltpu.VMEM((span, channels), BF16),
            pltpu.VMEM((span, channels), BF16),
            pltpu.VMEM((span, channels), BF16),
            pltpu.VMEM((16, channels), BF16),
            pltpu.VMEM((span + 8, channels), F32),
            pltpu.VMEM((span, channels), BF16),
            pltpu.VMEM((groups, piece, TB), BF16),
            pltpu.VMEM((2, pad + n * part, TB), BF16),
            pltpu.VMEM((2, pad + n * part, TB), BF16),
            pltpu.VMEM((groups, span // 128, 128), F32),
            pltpu.VMEM((seq // 128, 128), F32),
            pltpu.VMEM((seq // 128 + 1, 128, 128), BF16),
            pltpu.VMEM((n, piece, TB), BF16),
            pltpu.VMEM((groups, piece, TB), BF16),
            dma((3,)),
            dma((10,)),
            dma,
            dma,
            dma((3, n)),
            dma((3, n)),
            dma((n,)),
            dma((n,)),
            dma((3, 4)),
            dma((3, 4)),
        ],
        compiler_params=pltpu.CompilerParams(
            collective_id=0, has_side_effects=True, vmem_limit_bytes=62 << 20
        ),
    )(
        q_feat,
        k_feat,
        v_feat,
        short_taps,
        skip_bias.reshape(1, -1),
        freqs.reshape(1, -1),
        phases.reshape(1, -1),
        w_first,
        b_first.reshape(1, -1),
        w_second,
        b_second.reshape(1, -1),
        w_out.T,
        rates.reshape(1, -1),
    )


def solution(mesh):
    return jax.shard_map(
        on_device,
        mesh=mesh,
        in_specs=(
            P("ctx", "dp"),
            P("ctx", "dp"),
            P("ctx", "dp"),
            P(None, "dp"),
            P("dp"),
            P(),
            P(),
            P(),
            P(),
            P(),
            P(),
            P(None, "dp"),
            P("dp"),
        ),
        out_specs=P("ctx", "dp"),
        check_vma=False,
    )
```

```python
import functools
import math

import jax
import jax.numpy as jnp
from jax import lax
from jax.experimental import pallas as pl
from jax.experimental.pallas import tpu as pltpu
from jax.sharding import PartitionSpec as P

MESH = pl.DeviceIdType.MESH
F32 = jnp.float32
BF16 = jnp.bfloat16

TB = 256
CHAIN = 16
FAR = ((1, 2), (1, 1), (1, 3), (0, 2), (1, 0), (0, 1), (0, 3))

TURN_A = 6.28125
TURN_B = 0.001934051513671875
TURN_C = 1.2556658930407139e-06
TURN_BC = 0.0019353071693331003


def sine(x, small=False):
    turns = jnp.round(x * (0.5 / math.pi))
    r = x - turns * TURN_A
    if small:
        r = r - turns * TURN_BC
    else:
        r = (r - turns * TURN_B) - turns * TURN_C
    r2 = r * r
    tail = -2.4676328536088477e-08 + r2 * 1.3449288904787693e-10
    tail = 2.7529381441127043e-06 + r2 * tail
    tail = -0.00019840151071548462 + r2 * tail
    tail = 0.00833331048488617 + r2 * tail
    tail = -0.166666641831398 + r2 * tail
    return r + r * (r2 * tail)


def column(row):
    n = row.shape[1]
    square = jnp.broadcast_to(row, (n, n))
    at_row = lax.broadcasted_iota(jnp.int32, (n, n), 0)
    at_col = lax.broadcasted_iota(jnp.int32, (n, n), 1)
    return jnp.sum(jnp.where(at_row == at_col, square, 0.0), axis=1, keepdims=True)


def high_low(value):
    high = value.astype(BF16)
    return high, (value - high.astype(F32)).astype(BF16)


def stacked(weights):
    high, low = high_low(weights)
    return jnp.concatenate([high, high, low], 1)


def product(stack, value):
    high, low = high_low(value)
    return jnp.dot(
        stack, jnp.concatenate([high, low, high], 0), preferred_element_type=F32
    )


def kernel(
    n,
    span,
    groups,
    size,
    q_hbm,
    k_hbm,
    v_hbm,
    taps_hbm,
    skip_hbm,
    freqs_hbm,
    phases_hbm,
    w1_hbm,
    b1_hbm,
    w2_hbm,
    b2_hbm,
    wo_hbm,
    rates_hbm,
    o_ref,
    taps_ref,
    skip_ref,
    freqs_ref,
    phases_ref,
    w1_ref,
    b1_ref,
    w2_ref,
    b2_ref,
    wo_ref,
    rates_ref,
    q_ref,
    k_ref,
    v_ref,
    halo_ref,
    ext_ref,
    sig_ref,
    xs_ref,
    xe_ref,
    xo_ref,
    hs_ref,
    ha_ref,
    f_ref,
    ys_ref,
    yr_ref,
    in_sem,
    small_sem,
    halo_send,
    halo_recv,
    x_send,
    x_recv,
    h_send,
    h_recv,
    y_send,
    y_recv,
):
    me = lax.axis_index("ctx")
    seq = span * n
    blocks = span // TB
    rows = size // 2
    part = blocks * rows
    pad = CHAIN * rows

    side, place = me // 4, lax.rem(me, 4)

    def peer(step):
        return lax.rem(side + step[0], 2) * 4 + lax.rem(place + step[1], 4)

    def source(step):
        return lax.rem(side + step[0], 2) * 4 + lax.rem(place + 4 - step[1], 4)

    def slot(step):
        return step[0] * 4 + step[1]

    load_v = pltpu.make_async_copy(v_hbm, v_ref, in_sem.at[0])
    load_k = pltpu.make_async_copy(k_hbm, k_ref, in_sem.at[1])
    load_q = pltpu.make_async_copy(q_hbm, q_ref, in_sem.at[2])
    barrier = pltpu.get_barrier_semaphore()
    for step in FAR:
        pl.semaphore_signal(
            barrier, inc=1, device_id={"ctx": peer(step)}, device_id_type=MESH
        )
    load_v.start()
    load_k.start()
    loads = [
        pltpu.make_async_copy(src, dst, small_sem.at[i])
        for i, (src, dst) in enumerate(
            [
                (taps_hbm, taps_ref),
                (skip_hbm, skip_ref),
                (freqs_hbm, freqs_ref),
                (phases_hbm, phases_ref),
                (w1_hbm, w1_ref),
                (b1_hbm, b1_ref),
                (w2_hbm, w2_ref),
                (b2_hbm, b2_ref),
                (wo_hbm, wo_ref),
                (rates_hbm, rates_ref),
            ]
        )
    ]
    for load in loads:
        load.start()
    load_q.start()
    for h in range(2):
        xe_ref[h, 0:pad, :] = jnp.zeros((pad, TB), BF16)

    load_v.wait()
    pl.semaphore_wait(barrier, n - 1)
    halo = pltpu.make_async_remote_copy(
        src_ref=v_ref.at[pl.ds(span - 16, 16), :],
        dst_ref=halo_ref,
        send_sem=halo_send,
        recv_sem=halo_recv,
        device_id={"ctx": lax.rem(me + 1, n)},
        device_id_type=MESH,
    )
    halo.start()

    ext_ref[8:, :] = v_ref[...].astype(F32)
    for load in loads:
        load.wait()
    load_k.wait()
    taps = taps_ref[...]

    def one_pair(i, _):
        turned = []
        for u in range(2):
            at = pl.multiple_of((2 * i + u) * TB, TB)
            mixed = taps[0:1] * ext_ref[pl.ds(at + 8, TB), :]
            mixed = mixed + taps[1:2] * ext_ref[pl.ds(at + 7, TB), :]
            mixed = mixed + taps[2:3] * ext_ref[pl.ds(at + 6, TB), :]
            signal = (k_ref[pl.ds(at, TB), :].astype(F32) * mixed).astype(BF16)
            sig_ref[pl.ds(at, TB), :] = signal
            turned.append(signal.astype(F32).T)
        for g in range(groups):
            for h in range(2):
                low = g * size + h * rows
                row = pl.multiple_of(h * part + i * size, size)
                xs_ref[g, pl.ds(row, size), :] = jnp.concatenate(
                    [turned[0][low : low + rows], turned[1][low : low + rows]], 0
                ).astype(BF16)
        return 0

    for i in range(1, blocks // 2):
        one_pair(i, 0)

    parts = [(0, size, part - size), (0, 0, size), (1, 0, part)]

    def x_copy(step, p):
        h, first, count = parts[p]
        at = pl.multiple_of(pad + me * part + first, 16)
        return pltpu.make_async_remote_copy(
            src_ref=xs_ref.at[peer(step), pl.ds(h * part + first, count), :],
            dst_ref=xe_ref.at[h, pl.ds(at, count), :],
            send_sem=x_send.at[p, slot(step)],
            recv_sem=x_recv.at[p, slot(step)],
            device_id={"ctx": peer(step)},
            device_id_type=MESH,
        )

    def x_wait(step, p):
        h, first, count = parts[p]
        at = pl.multiple_of(pad + source(step) * part + first, 16)
        pltpu.make_async_remote_copy(
            src_ref=xs_ref.at[peer(step), pl.ds(h * part + first, count), :],
            dst_ref=xe_ref.at[h, pl.ds(at, count), :],
            send_sem=x_send.at[p, slot(step)],
            recv_sem=x_recv.at[p, slot(step)],
            device_id={"ctx": peer(step)},
            device_id_type=MESH,
        ).wait()

    for step in FAR:
        x_copy(step, 0).start()

    freq = column(freqs_ref[...]) * (2.0 * math.pi)
    phase = column(phases_ref[...])
    bias1 = column(b1_ref[...])
    bias2 = column(b2_ref[...])
    rate = column(rates_ref[...])
    layer1 = stacked(w1_ref[...].T)
    layer2 = stacked(w2_ref[...].T)
    layer3 = stacked(wo_ref[...])

    wide = span

    def some_positions(i):
        start = me * span + i * wide
        lanes = lax.broadcasted_iota(jnp.int32, (1, wide), 1) + start
        scaled = lanes.astype(F32) / seq
        feature = sine(freq * scaled + phase)
        first = sine(product(layer1, feature) + bias1, small=True)
        second = sine(product(layer2, first) + bias2, small=True)
        values = product(layer3, second) * jnp.exp(-rate * scaled)
        for t in range(wide // 128):
            for g in range(groups):
                hs_ref[g, pl.ds(i * (wide // 128) + t, 1), :] = values[
                    g : g + 1, t * 128 : (t + 1) * 128
                ]

    for i in range(span // wide):
        some_positions(i)

    tiles = span // 128

    def h_copy(step):
        return pltpu.make_async_remote_copy(
            src_ref=hs_ref.at[peer(step)],
            dst_ref=ha_ref.at[pl.ds(pl.multiple_of(me * tiles, 8), tiles), :],
            send_sem=h_send.at[slot(step)],
            recv_sem=h_recv.at[slot(step)],
            device_id={"ctx": peer(step)},
            device_id_type=MESH,
        )

    for step in FAR:
        h_copy(step).start()
    def h_wait(step):
        at = pl.multiple_of(source(step) * tiles, 8)
        pltpu.make_async_remote_copy(
            src_ref=hs_ref.at[peer(step)],
            dst_ref=ha_ref.at[pl.ds(at, tiles), :],
            send_sem=h_send.at[slot(step)],
            recv_sem=h_recv.at[slot(step)],
            device_id={"ctx": peer(step)},
            device_id_type=MESH,
        ).wait()

    halo.wait()
    ext_ref[0:8, :] = jnp.where(me > 0, halo_ref[8:16, :].astype(F32), 0.0)
    one_pair(0, 0)
    for step in FAR:
        x_copy(step, 1).start()
    for step in FAR:
        x_copy(step, 2).start()
    for h in range(2):
        at = pl.multiple_of(pad + me * part, 16)
        xe_ref[h, pl.ds(at, part), :] = xs_ref[me, h * part : (h + 1) * part, :]
    ha_ref[pl.ds(pl.multiple_of(me * tiles, 8), tiles), :] = hs_ref[me]

    at_row = lax.broadcasted_iota(jnp.int32, (128, 128), 0)
    at_col = lax.broadcasted_iota(jnp.int32, (128, 128), 1)
    keep = at_col >= at_row
    f_ref[0] = jnp.zeros((128, 128), BF16)

    def turned_row(at):
        row = jnp.broadcast_to(ha_ref[pl.ds(at, 1), :], (128, 128))
        return pltpu.roll(row, 0, 1, stride=1, stride_axis=0)

    for step in ((0, 0),) + FAR[::-1]:
        if step != (0, 0):
            h_wait(step)
        first = source(step) * tiles
        before = turned_row(first)
        for i in range(1, tiles):
            here = turned_row(first + i)
            f_ref[first + i + 1] = jnp.where(keep, here, before).astype(BF16)
            before = here
    for s in range(n):
        here = turned_row(s * tiles)
        if s == 0:
            before = jnp.zeros((128, 128), F32)
        else:
            before = turned_row(s * tiles - 1)
        f_ref[s * tiles + 1] = jnp.where(keep, here, before).astype(BF16)

    def lag_block(lag):
        low, mid, high = f_ref[2 * lag], f_ref[2 * lag + 1], f_ref[2 * lag + 2]
        return jnp.concatenate(
            [jnp.concatenate([mid, high], 1), jnp.concatenate([low, mid], 1)], 0
        )

    halves = [(0, part), (part, part), (0, 2 * part)]

    def y_copy(kind, to, other, index):
        first, count = halves[kind]
        return pltpu.make_async_remote_copy(
            src_ref=ys_ref.at[to, pl.ds(first, count), :],
            dst_ref=yr_ref.at[other, pl.ds(first, count), :],
            send_sem=y_send.at[kind, index],
            recv_sem=y_recv.at[kind, index],
            device_id={"ctx": to},
            device_id_type=MESH,
        )

    def shifted(h, start, count):
        if start % 16 == 0:
            return xe_ref[h, start : start + count, :]
        return xo_ref[h, start + rows : start + rows + count, :]

    def chain(halves_of, first, count, lags):
        left = [
            jnp.concatenate(
                [shifted(h, pad + first - lag * rows, count) for h in halves_of], 0
            )
            for lag in range(lags)
        ]
        right = [lag_block(lag) for lag in range(lags)]
        return jnp.dot(
            jnp.concatenate(left, 1),
            jnp.concatenate(right, 0),
            preferred_element_type=F32,
        ).astype(BF16)

    for h in range(2):
        for p in range(3):
            if parts[p][0] == h:
                for step in FAR[::-1]:
                    x_wait(step, p)
        count = pad + n * part
        xo_ref[h, 0:rows, :] = jnp.zeros((rows, TB), BF16)
        xo_ref[h, rows:count, :] = xe_ref[h, 0 : count - rows, :]

        for other in range(2):

            @pl.when(side == 1 - other)
            def _(other=other, h=h):
                for c in (4 * other + 2, 4 * other):
                    out = chain((h,), c * part, 2 * part, (c + 2) * blocks)
                    ys_ref[c, h * part : (h + 1) * part] = out[:part]
                    ys_ref[c + 1, h * part : (h + 1) * part] = out[part:]

        for move in (2, 1, 3, 0):
            y_copy(h, peer((1, move)), me, move).start()

    def one_span(i, _):
        move = (1 - i // 2) * (2 + i) + (i // 2) * (3 - i)
        to = side * 4 + lax.rem(place + move, 4)
        for c in range(n // 2, n):

            @pl.when(to == c)
            def _(c=c):
                ys_ref[c] = chain((0, 1), c * part, part, (c + 1) * blocks)

        @pl.when(i < 3)
        def _():
            y_copy(2, to, me, move).start()

        return 0

    @pl.when(side == 0)
    def _():
        for c in range(n // 2):
            ys_ref[c] = chain((0, 1), c * part, part, (c + 1) * blocks)
        for move in (2, 3, 1):
            y_copy(2, peer((0, move)), me, move).start()

    @pl.when(side == 1)
    def _():
        lax.fori_loop(0, 4, one_span, 0)

    yr_ref[me] = ys_ref[me]

    load_q.wait()
    for step in FAR:
        for kind in (0, 1) if step[0] else (2,):
            first, count = halves[kind]
            pltpu.make_async_remote_copy(
                src_ref=ys_ref.at[peer(step), pl.ds(first, count), :],
                dst_ref=yr_ref.at[source(step), pl.ds(first, count), :],
                send_sem=y_send.at[kind, step[1]],
                recv_sem=y_recv.at[kind, step[1]],
                device_id={"ctx": peer(step)},
                device_id_type=MESH,
            ).wait()

    skip = skip_ref[...]

    def last_pair(i, _):
        row = pl.multiple_of(i * size, size)
        two = [
            yr_ref[g, pl.ds(pl.multiple_of(h * part + row, 16), size), :].astype(F32)
            for g in range(groups)
            for h in range(2)
        ]
        for u in range(2):
            at = pl.multiple_of((2 * i + u) * TB, TB)
            conv = jnp.concatenate([x[u * rows : (u + 1) * rows] for x in two], 0).T
            total = conv + skip * sig_ref[pl.ds(at, TB), :].astype(F32)
            o_ref[pl.ds(at, TB), :] = (
                q_ref[pl.ds(at, TB), :].astype(F32) * total
            ).astype(BF16)
        return 0

    for i in range(blocks // 2):
        last_pair(i, 0)


def on_device(
    q_feat,
    k_feat,
    v_feat,
    short_taps,
    skip_bias,
    freqs,
    phases,
    w_first,
    b_first,
    w_second,
    b_second,
    w_out,
    rates,
):
    n = lax.axis_size("ctx")
    span, channels = q_feat.shape
    groups = rates.shape[0]
    size = channels // groups
    seq = span * n
    blocks = span // TB
    piece = blocks * size
    part = piece // 2
    pad = CHAIN * size // 2
    hbm = pl.BlockSpec(memory_space=pltpu.HBM)
    vmem = pl.BlockSpec(memory_space=pltpu.VMEM)
    dma = pltpu.SemaphoreType.DMA
    return pl.pallas_call(
        functools.partial(kernel, n, span, groups, size),
        name="toeplitz_conv",
        out_shape=pltpu.VMEM((span, channels), BF16),
        in_specs=[hbm] * 13,
        out_specs=vmem,
        scratch_shapes=[
            pltpu.VMEM(short_taps.shape, F32),
            pltpu.VMEM((1, channels), F32),
            pltpu.VMEM((1, freqs.shape[0]), F32),
            pltpu.VMEM((1, phases.shape[0]), F32),
            pltpu.VMEM(w_first.shape, F32),
            pltpu.VMEM((1, b_first.shape[0]), F32),
            pltpu.VMEM(w_second.shape, F32),
            pltpu.VMEM((1, b_second.shape[0]), F32),
            pltpu.VMEM((groups, w_out.shape[0]), F32),
            pltpu.VMEM((1, groups), F32),
            pltpu.VMEM((span, channels), BF16),
            pltpu.VMEM((span, channels), BF16),
            pltpu.VMEM((span, channels), BF16),
            pltpu.VMEM((16, channels), BF16),
            pltpu.VMEM((span + 8, channels), F32),
            pltpu.VMEM((span, channels), BF16),
            pltpu.VMEM((groups, piece, TB), BF16),
            pltpu.VMEM((2, pad + n * part, TB), BF16),
            pltpu.VMEM((2, pad + n * part, TB), BF16),
            pltpu.VMEM((groups, span // 128, 128), F32),
            pltpu.VMEM((seq // 128, 128), F32),
            pltpu.VMEM((seq // 128 + 1, 128, 128), BF16),
            pltpu.VMEM((n, piece, TB), BF16),
            pltpu.VMEM((groups, piece, TB), BF16),
            dma((3,)),
            dma((10,)),
            dma,
            dma,
            dma((3, n)),
            dma((3, n)),
            dma((n,)),
            dma((n,)),
            dma((3, 4)),
            dma((3, 4)),
        ],
        compiler_params=pltpu.CompilerParams(
            collective_id=0, has_side_effects=True, vmem_limit_bytes=62 << 20
        ),
    )(
        q_feat,
        k_feat,
        v_feat,
        short_taps,
        skip_bias.reshape(1, -1),
        freqs.reshape(1, -1),
        phases.reshape(1, -1),
        w_first,
        b_first.reshape(1, -1),
        w_second,
        b_second.reshape(1, -1),
        w_out.T,
        rates.reshape(1, -1),
    )


def solution(mesh):
    return jax.shard_map(
        on_device,
        mesh=mesh,
        in_specs=(
            P("ctx", "dp"),
            P("ctx", "dp"),
            P("ctx", "dp"),
            P(None, "dp"),
            P("dp"),
            P(),
            P(),
            P(),
            P(),
            P(),
            P(),
            P(None, "dp"),
            P("dp"),
        ),
        out_specs=P("ctx", "dp"),
        check_vma=False,
    )
```

```python
import functools
import math

import jax
import jax.numpy as jnp
from jax import lax
from jax.experimental import pallas as pl
from jax.experimental.pallas import tpu as pltpu
from jax.sharding import PartitionSpec as P

MESH = pl.DeviceIdType.MESH
F32 = jnp.float32
BF16 = jnp.bfloat16

TB = 256
CHAIN = 16
FAR = ((1, 2), (1, 1), (1, 3), (1, 0), (0, 2), (0, 1), (0, 3))

TURN_A = 6.28125
TURN_B = 0.001934051513671875
TURN_C = 1.2556658930407139e-06
TURN_BC = 0.0019353071693331003


def sine(x, small=False):
    turns = jnp.round(x * (0.5 / math.pi))
    r = x - turns * TURN_A
    if small:
        r = r - turns * TURN_BC
    else:
        r = (r - turns * TURN_B) - turns * TURN_C
    r2 = r * r
    tail = -2.4676328536088477e-08 + r2 * 1.3449288904787693e-10
    tail = 2.7529381441127043e-06 + r2 * tail
    tail = -0.00019840151071548462 + r2 * tail
    tail = 0.00833331048488617 + r2 * tail
    tail = -0.166666641831398 + r2 * tail
    return r + r * (r2 * tail)


def column(row):
    n = row.shape[1]
    square = jnp.broadcast_to(row, (n, n))
    at_row = lax.broadcasted_iota(jnp.int32, (n, n), 0)
    at_col = lax.broadcasted_iota(jnp.int32, (n, n), 1)
    return jnp.sum(jnp.where(at_row == at_col, square, 0.0), axis=1, keepdims=True)


def high_low(value):
    high = value.astype(BF16)
    return high, (value - high.astype(F32)).astype(BF16)


def stacked(weights):
    high, low = high_low(weights)
    return jnp.concatenate([high, high, low], 1)


def product(stack, value):
    high, low = high_low(value)
    return jnp.dot(
        stack, jnp.concatenate([high, low, high], 0), preferred_element_type=F32
    )


def kernel(
    n,
    span,
    groups,
    size,
    q_hbm,
    k_hbm,
    v_hbm,
    taps_hbm,
    skip_hbm,
    freqs_hbm,
    phases_hbm,
    w1_hbm,
    b1_hbm,
    w2_hbm,
    b2_hbm,
    wo_hbm,
    rates_hbm,
    o_ref,
    taps_ref,
    skip_ref,
    freqs_ref,
    phases_ref,
    w1_ref,
    b1_ref,
    w2_ref,
    b2_ref,
    wo_ref,
    rates_ref,
    q_ref,
    k_ref,
    v_ref,
    halo_ref,
    ext_ref,
    sig_ref,
    xs_ref,
    xe_ref,
    xo_ref,
    hs_ref,
    ha_ref,
    f_ref,
    ys_ref,
    yr_ref,
    in_sem,
    small_sem,
    halo_send,
    halo_recv,
    x_send,
    x_recv,
    h_send,
    h_recv,
    y_send,
    y_recv,
):
    me = lax.axis_index("ctx")
    seq = span * n
    blocks = span // TB
    rows = size // 2
    part = blocks * rows
    pad = CHAIN * rows

    side, place = me // 4, lax.rem(me, 4)

    def peer(step):
        return lax.rem(side + step[0], 2) * 4 + lax.rem(place + step[1], 4)

    def source(step):
        return lax.rem(side + step[0], 2) * 4 + lax.rem(place + 4 - step[1], 4)

    def slot(step):
        return step[0] * 4 + step[1]

    load_v = pltpu.make_async_copy(v_hbm, v_ref, in_sem.at[0])
    load_k = pltpu.make_async_copy(k_hbm, k_ref, in_sem.at[1])
    load_q = pltpu.make_async_copy(q_hbm, q_ref, in_sem.at[2])
    barrier = pltpu.get_barrier_semaphore()
    for step in FAR:
        pl.semaphore_signal(
            barrier, inc=1, device_id={"ctx": peer(step)}, device_id_type=MESH
        )
    load_v.start()
    load_k.start()
    loads = [
        pltpu.make_async_copy(src, dst, small_sem.at[i])
        for i, (src, dst) in enumerate(
            [
                (taps_hbm, taps_ref),
                (skip_hbm, skip_ref),
                (freqs_hbm, freqs_ref),
                (phases_hbm, phases_ref),
                (w1_hbm, w1_ref),
                (b1_hbm, b1_ref),
                (w2_hbm, w2_ref),
                (b2_hbm, b2_ref),
                (wo_hbm, wo_ref),
                (rates_hbm, rates_ref),
            ]
        )
    ]
    for load in loads:
        load.start()
    load_q.start()
    for h in range(2):
        xe_ref[h, 0:pad, :] = jnp.zeros((pad, TB), BF16)

    load_v.wait()
    pl.semaphore_wait(barrier, n - 1)
    halo = pltpu.make_async_remote_copy(
        src_ref=v_ref.at[pl.ds(span - 16, 16), :],
        dst_ref=halo_ref,
        send_sem=halo_send,
        recv_sem=halo_recv,
        device_id={"ctx": lax.rem(me + 1, n)},
        device_id_type=MESH,
    )
    halo.start()

    ext_ref[8:, :] = v_ref[...].astype(F32)
    for load in loads:
        load.wait()
    load_k.wait()
    taps = taps_ref[...]

    def one_pair(i, _):
        turned = []
        for u in range(2):
            at = pl.multiple_of((2 * i + u) * TB, TB)
            mixed = taps[0:1] * ext_ref[pl.ds(at + 8, TB), :]
            mixed = mixed + taps[1:2] * ext_ref[pl.ds(at + 7, TB), :]
            mixed = mixed + taps[2:3] * ext_ref[pl.ds(at + 6, TB), :]
            signal = (k_ref[pl.ds(at, TB), :].astype(F32) * mixed).astype(BF16)
            sig_ref[pl.ds(at, TB), :] = signal
            turned.append(signal.astype(F32).T)
        for g in range(groups):
            for h in range(2):
                low = g * size + h * rows
                row = pl.multiple_of(h * part + i * size, size)
                xs_ref[g, pl.ds(row, size), :] = jnp.concatenate(
                    [turned[0][low : low + rows], turned[1][low : low + rows]], 0
                ).astype(BF16)
        return 0

    for i in range(1, blocks // 2):
        one_pair(i, 0)

    parts = [(0, size, part - size), (0, 0, size), (1, 0, part)]

    def x_copy(step, p):
        h, first, count = parts[p]
        at = pl.multiple_of(pad + me * part + first, 16)
        return pltpu.make_async_remote_copy(
            src_ref=xs_ref.at[peer(step), pl.ds(h * part + first, count), :],
            dst_ref=xe_ref.at[h, pl.ds(at, count), :],
            send_sem=x_send.at[p, slot(step)],
            recv_sem=x_recv.at[p, slot(step)],
            device_id={"ctx": peer(step)},
            device_id_type=MESH,
        )

    def x_wait(step, p):
        h, first, count = parts[p]
        at = pl.multiple_of(pad + source(step) * part + first, 16)
        pltpu.make_async_remote_copy(
            src_ref=xs_ref.at[peer(step), pl.ds(h * part + first, count), :],
            dst_ref=xe_ref.at[h, pl.ds(at, count), :],
            send_sem=x_send.at[p, slot(step)],
            recv_sem=x_recv.at[p, slot(step)],
            device_id={"ctx": peer(step)},
            device_id_type=MESH,
        ).wait()

    for step in FAR:
        x_copy(step, 0).start()

    freq = column(freqs_ref[...]) * (2.0 * math.pi)
    phase = column(phases_ref[...])
    bias1 = column(b1_ref[...])
    bias2 = column(b2_ref[...])
    rate = column(rates_ref[...])
    layer1 = stacked(w1_ref[...].T)
    layer2 = stacked(w2_ref[...].T)
    layer3 = stacked(wo_ref[...])

    wide = span

    def some_positions(i):
        start = me * span + i * wide
        lanes = lax.broadcasted_iota(jnp.int32, (1, wide), 1) + start
        scaled = lanes.astype(F32) / seq
        feature = sine(freq * scaled + phase)
        first = sine(product(layer1, feature) + bias1, small=True)
        second = sine(product(layer2, first) + bias2, small=True)
        values = product(layer3, second) * jnp.exp(-rate * scaled)
        for t in range(wide // 128):
            for g in range(groups):
                hs_ref[g, pl.ds(i * (wide // 128) + t, 1), :] = values[
                    g : g + 1, t * 128 : (t + 1) * 128
                ]

    for i in range(span // wide):
        some_positions(i)

    tiles = span // 128

    def h_copy(step):
        return pltpu.make_async_remote_copy(
            src_ref=hs_ref.at[peer(step)],
            dst_ref=ha_ref.at[pl.ds(pl.multiple_of(me * tiles, 8), tiles), :],
            send_sem=h_send.at[slot(step)],
            recv_sem=h_recv.at[slot(step)],
            device_id={"ctx": peer(step)},
            device_id_type=MESH,
        )

    for step in FAR:
        h_copy(step).start()
    def h_wait(step):
        at = pl.multiple_of(source(step) * tiles, 8)
        pltpu.make_async_remote_copy(
            src_ref=hs_ref.at[peer(step)],
            dst_ref=ha_ref.at[pl.ds(at, tiles), :],
            send_sem=h_send.at[slot(step)],
            recv_sem=h_recv.at[slot(step)],
            device_id={"ctx": peer(step)},
            device_id_type=MESH,
        ).wait()

    halo.wait()
    ext_ref[0:8, :] = jnp.where(me > 0, halo_ref[8:16, :].astype(F32), 0.0)
    one_pair(0, 0)
    for step in FAR:
        x_copy(step, 1).start()
    for step in FAR:
        x_copy(step, 2).start()
    for h in range(2):
        at = pl.multiple_of(pad + me * part, 16)
        xe_ref[h, pl.ds(at, part), :] = xs_ref[me, h * part : (h + 1) * part, :]
    ha_ref[pl.ds(pl.multiple_of(me * tiles, 8), tiles), :] = hs_ref[me]

    at_row = lax.broadcasted_iota(jnp.int32, (128, 128), 0)
    at_col = lax.broadcasted_iota(jnp.int32, (128, 128), 1)
    keep = at_col >= at_row
    f_ref[0] = jnp.zeros((128, 128), BF16)

    def turned_row(at):
        row = jnp.broadcast_to(ha_ref[pl.ds(at, 1), :], (128, 128))
        return pltpu.roll(row, 0, 1, stride=1, stride_axis=0)

    for step in ((0, 0),) + FAR[::-1]:
        if step != (0, 0):
            h_wait(step)
        first = source(step) * tiles
        before = turned_row(first)
        for i in range(1, tiles):
            here = turned_row(first + i)
            f_ref[first + i + 1] = jnp.where(keep, here, before).astype(BF16)
            before = here
    for s in range(n):
        here = turned_row(s * tiles)
        if s == 0:
            before = jnp.zeros((128, 128), F32)
        else:
            before = turned_row(s * tiles - 1)
        f_ref[s * tiles + 1] = jnp.where(keep, here, before).astype(BF16)

    def lag_block(lag):
        low, mid, high = f_ref[2 * lag], f_ref[2 * lag + 1], f_ref[2 * lag + 2]
        return jnp.concatenate(
            [jnp.concatenate([mid, high], 1), jnp.concatenate([low, mid], 1)], 0
        )

    halves = [(0, part), (part, part), (0, 2 * part)]

    def y_copy(kind, to, other, index):
        first, count = halves[kind]
        return pltpu.make_async_remote_copy(
            src_ref=ys_ref.at[to, pl.ds(first, count), :],
            dst_ref=yr_ref.at[other, pl.ds(first, count), :],
            send_sem=y_send.at[kind, index],
            recv_sem=y_recv.at[kind, index],
            device_id={"ctx": to},
            device_id_type=MESH,
        )

    def shifted(h, start, count):
        if start % 16 == 0:
            return xe_ref[h, start : start + count, :]
        return xo_ref[h, start + rows : start + rows + count, :]

    def chain(halves_of, first, count, lags):
        left = [
            jnp.concatenate(
                [shifted(h, pad + first - lag * rows, count) for h in halves_of], 0
            )
            for lag in range(lags)
        ]
        right = [lag_block(lag) for lag in range(lags)]
        return jnp.dot(
            jnp.concatenate(left, 1),
            jnp.concatenate(right, 0),
            preferred_element_type=F32,
        ).astype(BF16)

    for h in range(2):
        for p in range(3):
            if parts[p][0] == h:
                for step in FAR[::-1]:
                    x_wait(step, p)
        count = pad + n * part
        xo_ref[h, 0:rows, :] = jnp.zeros((rows, TB), BF16)
        xo_ref[h, rows:count, :] = xe_ref[h, 0 : count - rows, :]

        for other in range(2):

            @pl.when(side == 1 - other)
            def _(other=other, h=h):
                for c in (4 * other + 2, 4 * other):
                    out = chain((h,), c * part, 2 * part, (c + 2) * blocks)
                    ys_ref[c, h * part : (h + 1) * part] = out[:part]
                    ys_ref[c + 1, h * part : (h + 1) * part] = out[part:]

        for move in (2, 1, 3, 0):
            y_copy(h, peer((1, move)), me, move).start()

    def one_span(i, _):
        move = (1 - i // 2) * (2 + i) + (i // 2) * (3 - i)
        to = side * 4 + lax.rem(place + move, 4)
        for c in range(n // 2, n):

            @pl.when(to == c)
            def _(c=c):
                ys_ref[c] = chain((0, 1), c * part, part, (c + 1) * blocks)

        @pl.when(i < 3)
        def _():
            y_copy(2, to, me, move).start()

        return 0

    @pl.when(side == 0)
    def _():
        for c in range(n // 2):
            ys_ref[c] = chain((0, 1), c * part, part, (c + 1) * blocks)
        for move in (2, 3, 1):
            y_copy(2, peer((0, move)), me, move).start()

    @pl.when(side == 1)
    def _():
        lax.fori_loop(0, 4, one_span, 0)

    yr_ref[me] = ys_ref[me]

    load_q.wait()
    for step in FAR:
        for kind in (0, 1) if step[0] else (2,):
            first, count = halves[kind]
            pltpu.make_async_remote_copy(
                src_ref=ys_ref.at[peer(step), pl.ds(first, count), :],
                dst_ref=yr_ref.at[source(step), pl.ds(first, count), :],
                send_sem=y_send.at[kind, step[1]],
                recv_sem=y_recv.at[kind, step[1]],
                device_id={"ctx": peer(step)},
                device_id_type=MESH,
            ).wait()

    skip = skip_ref[...]

    def last_pair(i, _):
        row = pl.multiple_of(i * size, size)
        two = [
            yr_ref[g, pl.ds(pl.multiple_of(h * part + row, 16), size), :].astype(F32)
            for g in range(groups)
            for h in range(2)
        ]
        for u in range(2):
            at = pl.multiple_of((2 * i + u) * TB, TB)
            conv = jnp.concatenate([x[u * rows : (u + 1) * rows] for x in two], 0).T
            total = conv + skip * sig_ref[pl.ds(at, TB), :].astype(F32)
            o_ref[pl.ds(at, TB), :] = (
                q_ref[pl.ds(at, TB), :].astype(F32) * total
            ).astype(BF16)
        return 0

    for i in range(blocks // 2):
        last_pair(i, 0)


def on_device(
    q_feat,
    k_feat,
    v_feat,
    short_taps,
    skip_bias,
    freqs,
    phases,
    w_first,
    b_first,
    w_second,
    b_second,
    w_out,
    rates,
):
    n = lax.axis_size("ctx")
    span, channels = q_feat.shape
    groups = rates.shape[0]
    size = channels // groups
    seq = span * n
    blocks = span // TB
    piece = blocks * size
    part = piece // 2
    pad = CHAIN * size // 2
    hbm = pl.BlockSpec(memory_space=pltpu.HBM)
    vmem = pl.BlockSpec(memory_space=pltpu.VMEM)
    dma = pltpu.SemaphoreType.DMA
    return pl.pallas_call(
        functools.partial(kernel, n, span, groups, size),
        name="toeplitz_conv",
        out_shape=pltpu.VMEM((span, channels), BF16),
        in_specs=[hbm] * 13,
        out_specs=vmem,
        scratch_shapes=[
            pltpu.VMEM(short_taps.shape, F32),
            pltpu.VMEM((1, channels), F32),
            pltpu.VMEM((1, freqs.shape[0]), F32),
            pltpu.VMEM((1, phases.shape[0]), F32),
            pltpu.VMEM(w_first.shape, F32),
            pltpu.VMEM((1, b_first.shape[0]), F32),
            pltpu.VMEM(w_second.shape, F32),
            pltpu.VMEM((1, b_second.shape[0]), F32),
            pltpu.VMEM((groups, w_out.shape[0]), F32),
            pltpu.VMEM((1, groups), F32),
            pltpu.VMEM((span, channels), BF16),
            pltpu.VMEM((span, channels), BF16),
            pltpu.VMEM((span, channels), BF16),
            pltpu.VMEM((16, channels), BF16),
            pltpu.VMEM((span + 8, channels), F32),
            pltpu.VMEM((span, channels), BF16),
            pltpu.VMEM((groups, piece, TB), BF16),
            pltpu.VMEM((2, pad + n * part, TB), BF16),
            pltpu.VMEM((2, pad + n * part, TB), BF16),
            pltpu.VMEM((groups, span // 128, 128), F32),
            pltpu.VMEM((seq // 128, 128), F32),
            pltpu.VMEM((seq // 128 + 1, 128, 128), BF16),
            pltpu.VMEM((n, piece, TB), BF16),
            pltpu.VMEM((groups, piece, TB), BF16),
            dma((3,)),
            dma((10,)),
            dma,
            dma,
            dma((3, n)),
            dma((3, n)),
            dma((n,)),
            dma((n,)),
            dma((3, 4)),
            dma((3, 4)),
        ],
        compiler_params=pltpu.CompilerParams(
            collective_id=0, has_side_effects=True, vmem_limit_bytes=62 << 20
        ),
    )(
        q_feat,
        k_feat,
        v_feat,
        short_taps,
        skip_bias.reshape(1, -1),
        freqs.reshape(1, -1),
        phases.reshape(1, -1),
        w_first,
        b_first.reshape(1, -1),
        w_second,
        b_second.reshape(1, -1),
        w_out.T,
        rates.reshape(1, -1),
    )


def solution(mesh):
    return jax.shard_map(
        on_device,
        mesh=mesh,
        in_specs=(
            P("ctx", "dp"),
            P("ctx", "dp"),
            P("ctx", "dp"),
            P(None, "dp"),
            P("dp"),
            P(),
            P(),
            P(),
            P(),
            P(),
            P(),
            P(None, "dp"),
            P("dp"),
        ),
        out_specs=P("ctx", "dp"),
        check_vma=False,
    )
```
